32 devices in a mesh: tm: 8 (over y, x, core), space: 4 (over z).
Axes of the slice: x: 2, y: 2, z: 4, core: 2. Of those that a mesh axis runs over, the one named last changes fastest.
Arguments:
- start_block: float32 [16, 32, 8192], P('tm', None, 'space'), as said below
- stiffness_tiles: float32 [16, 320, 128, 128], P('tm', 'space'), as said below
- tile_columns: int32 [16, 320], P('tm', 'space'), may hold values from 0 to 63, as said below
Outputs:
- ritz_basis: float32 [16, 32, 8192], P('tm', None, 'space')
- first_basis: float32 [16, 32, 8192], P('tm', None, 'space')
- ritz_matrix: float32 [32, 32], replicated
The draws below stay inside these ranges and needn't reach their ends.
Inputs may be any that keep to these rules, and one draw needn't show every extreme that they name: `tile_columns`: in every slice, block row r has its 5 tiles listed together in row order; the first names column block r, the others distinct column blocks (r + o) mod 64 with 0 < |o| <= 8; in every slice some block row has o = -8 and o = 8. `stiffness_tiles`: real entries. `start_block`: real entries.
All inputs are finite; a program needn't handle non-finite values.
Results may differ from the reference program's by a relative error of at most 0.00018.
Values sent between devices are 32-bit elements; how exact they have to be, the bound alone decides.
No kernel may reach another device: no remote copies, remote signals or barrier semaphores. Data moves between devices by JAX's collectives and lax.ppermute only.
A program may use at most 192 MiB of HBM per device.

```python
import math
import jax
import jax.numpy as jnp
from jax import lax

TILE = 128
VECS = 32
TPR = 5
HB = 8
SLICES = 16
NB = 64
NPTS = 8192
NTOTAL = 131072


def draw_start_block(key, part):
    shape = (SLICES, VECS, NPTS)
    key_main = jax.random.fold_in(jax.random.fold_in(key, 5), 0)
    slice_pos = jnp.arange(SLICES, dtype=jnp.float32) / max(SLICES - 1, 1)
    point_pos = jnp.arange(NPTS, dtype=jnp.float32) / max(NPTS - 1, 1)
    base = jax.random.normal(key_main, shape, jnp.float32)
    slice_scale = 1.0 + 2.0 * slice_pos
    point_scale = 1.0 + 2.0 * point_pos
    return base * slice_scale[:, None, None] * point_scale[None, None, :]


def draw_stiffness_tiles(key, part):
    key_noise, key_diag = jax.random.split(jax.random.fold_in(key, 3))
    shape = (SLICES, NB * TPR, TILE, TILE)
    sigma = 0.8 / math.sqrt(TPR * TILE)
    noise = jax.random.normal(key_noise, shape, jnp.float32) * sigma
    diag_values = jax.random.uniform(key_diag, (SLICES, NB * TPR, TILE), jnp.float32, 2.0, 4.0)
    leading = (jnp.arange(NB * TPR) % TPR == 0).astype(jnp.float32)
    identity = jnp.eye(TILE, dtype=jnp.float32)
    return noise + (leading[None, :, None] * diag_values)[:, :, :, None] * identity


def draw_tile_columns(key, part):
    row_count = SLICES * NB
    row_keys = jax.random.split(jax.random.fold_in(key, 7), row_count)
    offsets_all = jnp.concatenate([jnp.arange(-HB, 0), jnp.arange(1, HB + 1)]).astype(jnp.int32)
    offsets_inner = jnp.concatenate([jnp.arange(-HB + 1, 0), jnp.arange(1, HB)]).astype(jnp.int32)

    def one_row(row_key):
        drawn = jax.random.permutation(row_key, offsets_all)[:TPR - 1]
        inner = jax.random.permutation(jax.random.fold_in(row_key, 1), offsets_inner)[:TPR - 3]
        return (drawn, inner)
    drawn_picks, inner_picks = jax.vmap(one_row)(row_keys)
    forced = jnp.concatenate([jnp.full((row_count, 1), -HB, jnp.int32), jnp.full((row_count, 1), HB, jnp.int32), inner_picks], axis=1)
    chosen_row = jax.random.randint(jax.random.fold_in(key, 11), (SLICES,), 0, NB)
    is_forced = (jnp.arange(NB)[None, :] == chosen_row[:, None]).reshape(row_count)
    offsets = jnp.where(is_forced[:, None], forced, drawn_picks)
    offsets = jnp.concatenate([jnp.zeros((row_count, 1), jnp.int32), offsets], axis=1)
    row_index = jnp.tile(jnp.arange(NB, dtype=jnp.int32), SLICES)
    columns = (row_index[:, None] + offsets) % NB
    return columns.reshape(SLICES, NB * TPR).astype(jnp.int32)


def setup_inputs(seed: int = 0) -> dict:
    arg_keys = jax.random.split(jax.random.key(seed), 4)
    return {
        "start_block": draw_start_block(jax.random.fold_in(arg_keys[3], 71), 0),
        "stiffness_tiles": draw_stiffness_tiles(jax.random.fold_in(arg_keys[3], 71), 0),
        "tile_columns": draw_tile_columns(jax.random.fold_in(arg_keys[3], 71), 0),
    }


CENTER = 6.5
RADIUS = 3.5
INFLATION_FACTOR = 0.8
accurate = lax.Precision.HIGHEST

def apply_operator(vectors, tile_groups, column_groups, degree):
    slices, width, points = vectors.shape
    blocks = points // TILE

    def one_slice(items):
        slice_vec, tile_set, col_list = items
        picked = jnp.take(slice_vec.reshape(width, blocks, TILE), col_list, axis=1)
        products = jnp.einsum('nrc,knc->knr', tile_set, picked, precision=accurate)
        return products.reshape(width, blocks, TPR, TILE).sum(axis=2).reshape(width, points)
    spatial_operator = lax.map(one_slice, (vectors, tile_groups, column_groups))
    padded = jnp.pad(vectors, ((1, 1), (0, 0), (0, 0)))
    temporal_operator = degree[:, None, None] * vectors - padded[:-2] - padded[2:]
    return spatial_operator + INFLATION_FACTOR * temporal_operator

def chebyshev_filter(vectors, operator):
    previous = vectors
    current = (operator(vectors) - CENTER * vectors) / RADIUS
    for step in range(2):
        following = 2.0 * (operator(current) - CENTER * current) / RADIUS - previous
        previous, current = (current, following)
    return current

def gram_terms(left_block, right_block):
    return jnp.einsum('sjp,skp->jk', left_block, right_block, precision=accurate)

def inverse_factor(gram_matrix):
    cholesky_factor = jnp.linalg.cholesky(gram_matrix)
    identity = jnp.eye(gram_matrix.shape[0], dtype=jnp.float32)
    return lax.linalg.triangular_solve(cholesky_factor, identity, left_side=True, lower=True)

def mix_vectors(matrix, vectors):
    return jnp.einsum('jk,skp->sjp', matrix, vectors, precision=accurate)

def reference(start_block, stiffness_tiles, tile_columns):
    slice_index = jnp.arange(SLICES, dtype=jnp.int32)
    degree = 2.0 - (slice_index == 0).astype(jnp.float32) - (slice_index == SLICES - 1).astype(jnp.float32)

    def operator(vectors):
        return apply_operator(vectors, stiffness_tiles, tile_columns, degree)
    filtered = chebyshev_filter(start_block, operator)
    first_basis = mix_vectors(inverse_factor(gram_terms(filtered, filtered) / NTOTAL), filtered)
    second = chebyshev_filter(first_basis, operator)
    ritz_basis = mix_vectors(inverse_factor(gram_terms(second, second) / NTOTAL), second)
    image_block = operator(ritz_basis)
    ritz_matrix = gram_terms(ritz_basis, image_block) / NTOTAL
    return (ritz_basis, first_basis, ritz_matrix)
```

```python
import functools

import jax
import jax.numpy as jnp
from jax import lax
from jax.experimental import pallas as pl
from jax.experimental.pallas import tpu as pltpu
from jax.sharding import PartitionSpec as P

TILE = 128
TPR = 5
HB = 8
CENTER = 6.5
RADIUS = 3.5
INFLATION_FACTOR = 0.8

F32 = jnp.float32
BF16 = jnp.bfloat16
VM = pltpu.VMEM
NT = (((1,), (1,)), ((), ()))
NN = (((1,), (0,)), ((), ()))
WHOLE = pl.BlockSpec(memory_space=VM)
SCALARS = pl.BlockSpec(memory_space=pltpu.SMEM)


def near(x):
    return pltpu.with_memory_space_constraint(x, VM)


def split(x):
    high = x.astype(BF16)
    return high, (x - high.astype(F32)).astype(BF16)


def stacked(x):
    return jnp.concatenate(split(x), axis=0)


def call(kernel, ins, outs, scratch=(), specs=None, flops=0, moved=0, name=None, out_vmem=True):
    out_shape = [VM(s, d) if out_vmem else jax.ShapeDtypeStruct(s, d) for s, d in outs]
    return pl.pallas_call(
        kernel,
        out_shape=out_shape,
        in_specs=specs,
        out_specs=[WHOLE] * len(outs),
        scratch_shapes=list(scratch),
        name=name,
        cost_estimate=pl.CostEstimate(flops=flops, bytes_accessed=moved, transcendentals=0),
        compiler_params=pltpu.CompilerParams(vmem_limit_bytes=48 << 20),
    )(*ins)


def prep_kernel(tiles_ref, out_ref):
    high, low = split(tiles_ref[...])
    out_ref[:, :, :TILE, :] = high
    out_ref[:, :, TILE:, :] = low


def prep(tiles):
    slices, count = tiles.shape[:2]
    step = 16
    return pl.pallas_call(
        prep_kernel,
        grid=(slices, count // step),
        out_shape=VM((slices, count, 2 * TILE, TILE), BF16),
        in_specs=[pl.BlockSpec((1, step, TILE, TILE), lambda s, i: (s, i, 0, 0))],
        out_specs=pl.BlockSpec((1, step, 2 * TILE, TILE), lambda s, i: (s, i, 0, 0)),
        name="prep",
        cost_estimate=pl.CostEstimate(
            flops=0, bytes_accessed=2 * 4 * tiles.size, transcendentals=0
        ),
        compiler_params=pltpu.CompilerParams(vmem_limit_bytes=32 << 20),
    )(tiles)


def edges(y_ref, head_ref, tail_ref, first_ref, last_ref):
    width = HB * TILE
    points = y_ref.shape[2]
    head_ref[...] = y_ref[:, :, :width]
    tail_ref[...] = y_ref[:, :, points - width :]
    first_ref[...] = y_ref[:1]
    last_ref[...] = y_ref[y_ref.shape[0] - 1 :]


def edge_shapes(shape):
    slices, width, points = shape
    side = (slices, width, HB * TILE)
    return [(shape, F32), (side, F32), (side, F32), ((1, width, points), F32), ((1, width, points), F32)]


def start_kernel(x_ref, y_ref, *edge_refs):
    y_ref[...] = x_ref[...]
    edges(y_ref, *edge_refs)


def start(block):
    return call(
        start_kernel, [block], edge_shapes(block.shape), specs=[WHOLE], moved=16 * block.size, name="start"
    )


def matmul_tile(lhs, tile):
    return lax.dot_general(lhs, tile, NT, preferred_element_type=F32)


def fold(product, width):
    return product[:width, :TILE] + product[:width, TILE:] + product[width:, :TILE]


def local_kernel(place_ref, tiles_ref, y_ref, out_ref, halves_ref):
    slices, width, points = y_ref.shape
    blocks = points // TILE
    for s in range(slices):
        for b in range(blocks):
            halves_ref[s, b] = stacked(y_ref[s, :, b * TILE : (b + 1) * TILE])
        halves_ref[s, blocks] = jnp.zeros((2 * width, TILE), BF16)

    def row(i, carry):
        s, r = i // blocks, i % blocks
        total = None
        for n in range(TPR):
            where = place_ref[s, r * TPR + n] - HB
            inside = jnp.logical_and(where >= 0, where < blocks)
            where = jnp.where(inside, where, blocks)
            term = matmul_tile(halves_ref[s, where], tiles_ref[s, r * TPR + n])
            total = term if total is None else total + term
        out_ref[s, :, pl.ds(pl.multiple_of(r * TILE, TILE), TILE)] = fold(total, width)
        return carry

    lax.fori_loop(0, slices * blocks, row, 0, unroll=4)


def local_part(place, tiles, y):
    slices, width, points = y.shape
    blocks = points // TILE
    return call(
        local_kernel,
        [place, near(tiles), near(y)],
        [(y.shape, F32)],
        specs=[SCALARS, WHOLE, WHOLE],
        scratch=[VM((slices, blocks + 1, 2 * width, TILE), BF16)],
        flops=2 * slices * blocks * TPR * 4 * width * TILE * TILE,
        moved=8 * y.size,
        name="local",
    )[0]


def mix(matrix, y):
    high, low = split(matrix)
    y_high, y_low = split(y)
    left = jnp.concatenate([high, low, high], axis=1)
    right = jnp.concatenate([y_high, y_high, y_low], axis=0)
    return lax.dot_general(left, right, NN, preferred_element_type=F32)


def inner(left, right):
    width = left.shape[0]
    p = lax.dot_general(stacked(left), stacked(right), NT, preferred_element_type=F32)
    return (p[:width, :width] + p[width:, width:]) + (p[:width, width:] + p[width:, :width])


def finish_kernel(mode, scale, *refs):
    refs = list(refs)
    take = lambda n: [refs.pop(0) for _ in range(n)]
    place_ref, degree_ref, tiles_ref, part_ref, y_ref = take(5)
    left_ref, right_ref, before_ref, after_ref = take(4)
    previous_ref = take(1)[0] if mode in ("step", "gram", "mixed") else None
    matrix_ref = take(1)[0] if mode == "mixed" else None
    if mode == "image":
        (gram_ref,) = take(1)
    else:
        new_ref, *edge_refs = take(5)
        gram_ref = take(1)[0] if mode in ("gram", "mixed") else None
    halves_ref = take(1)[0]
    if mode == "image":
        new_ref = take(1)[0]
    slices, width, points = y_ref.shape
    blocks = points // TILE
    for s in range(slices):
        for b in range(HB):
            halves_ref[s, b] = stacked(left_ref[s, :, b * TILE : (b + 1) * TILE])
            halves_ref[s, HB + b] = stacked(right_ref[s, :, b * TILE : (b + 1) * TILE])
        halves_ref[s, 2 * HB] = jnp.zeros((2 * width, TILE), BF16)

    for s in range(slices):

        def row(r, carry, s=s):
            total = None
            for n in range(1, TPR):
                where = place_ref[s, r * TPR + n]
                right = where >= HB + blocks
                where = jnp.where(right, where - blocks, jnp.where(where < HB, where, 2 * HB))
                term = matmul_tile(halves_ref[s, where], tiles_ref[s, r * TPR + n])
                total = term if total is None else total + term
            here = pl.ds(pl.multiple_of(r * TILE, TILE), TILE)
            y = y_ref[s, :, here]
            before = before_ref[0, :, here] if s == 0 else y_ref[s - 1, :, here]
            after = after_ref[0, :, here] if s == slices - 1 else y_ref[s + 1, :, here]
            image = part_ref[s, :, here] + fold(total, width)
            image = image + INFLATION_FACTOR * (degree_ref[s] * y - before - after)
            if mode != "image":
                image = (image - CENTER * y) * scale
                if previous_ref is not None:
                    image = image - previous_ref[s, :, here]
            new_ref[s, :, here] = image
            return carry

        lax.fori_loop(0, blocks, row, 0, unroll=4)

    if mode == "mixed":
        for s in range(slices):
            new_ref[s] = mix(matrix_ref[...], new_ref[s])
    if mode != "image":
        edges(new_ref, *edge_refs)
    if gram_ref is not None:
        base_ref = y_ref if mode == "image" else new_ref
        total = inner(base_ref[0], new_ref[0])
        for s in range(1, slices):
            total = total + inner(base_ref[s], new_ref[s])
        gram_ref[...] = total


def finish(mode, scale, place, degree, tiles, part, y, halo, previous=None, matrix=None):
    slices, width, points = y.shape
    blocks = points // TILE
    ins = [place, degree] + [near(v) for v in (tiles, part, y, *halo)]
    specs = [SCALARS, SCALARS] + [WHOLE] * 7
    for extra in (previous, matrix):
        if extra is not None:
            ins.append(near(extra))
            specs.append(WHOLE)
    outs = [] if mode == "image" else edge_shapes(y.shape)
    if mode in ("gram", "mixed", "image"):
        outs = outs + [((width, width), F32)]
    scratch = [VM((slices, 2 * HB + 1, 2 * width, TILE), BF16)]
    if mode == "image":
        scratch.append(VM(y.shape, F32))
    return call(
        functools.partial(finish_kernel, mode, scale),
        ins,
        outs,
        scratch=scratch,
        specs=specs,
        flops=2 * slices * blocks * TPR * 4 * width * TILE * TILE,
        moved=24 * y.size,
        name="finish_" + mode,
    )


def inverse_factor(gram):
    width = gram.shape[0]
    rows = lax.broadcasted_iota(jnp.int32, (width, width), 0)
    columns = lax.broadcasted_iota(jnp.int32, (width, width), 1)
    inverse = (rows == columns).astype(F32)
    row_of = lax.broadcasted_iota(jnp.int32, (width, 1), 0)
    for j in range(width):
        root = lax.rsqrt(gram[j : j + 1, j : j + 1])
        gram_row = gram[j : j + 1, :] * root
        inverse_row = inverse[j : j + 1, :] * root
        column = jnp.where(row_of > j, gram[:, j : j + 1] * root, 0.0)
        gram = gram - column * gram_row
        inverse = jnp.where(row_of == j, inverse_row, inverse - column * inverse_row)
    return inverse


def orth_kernel(count, gram_ref, y_ref, out_ref, matrix_ref):
    matrix = inverse_factor(gram_ref[...] * (1.0 / count))
    matrix_ref[...] = matrix
    for s in range(y_ref.shape[0]):
        out_ref[s] = mix(matrix, y_ref[s])


def orth(gram, y, count):
    width = gram.shape[0]
    return pl.pallas_call(
        functools.partial(orth_kernel, float(count)),
        out_shape=[jax.ShapeDtypeStruct(y.shape, F32), VM((width, width), F32)],
        in_specs=[WHOLE, WHOLE],
        out_specs=[WHOLE, WHOLE],
        name="orth",
        cost_estimate=pl.CostEstimate(flops=2 * width * y.size, bytes_accessed=8 * y.size, transcendentals=0),
        compiler_params=pltpu.CompilerParams(vmem_limit_bytes=16 << 20),
    )(near(gram), near(y))


def ritz_kernel(count, matrix_ref, inner_ref, out_ref):
    high = lax.Precision.HIGHEST
    matrix = matrix_ref[...]
    half = lax.dot_general(matrix, inner_ref[...] * (1.0 / count), NN, precision=high, preferred_element_type=F32)
    out_ref[...] = lax.dot_general(half, matrix, NT, precision=high, preferred_element_type=F32)


def ritz(matrix, product, count):
    return call(
        functools.partial(ritz_kernel, float(count)),
        [near(matrix), near(product)],
        [(product.shape, F32)],
        specs=[WHOLE, WHOLE],
        name="ritz",
        moved=4 * product.size,
        out_vmem=False,
    )[0]


def total_over(value, axis):
    count = lax.axis_size(axis)
    stride = 1
    while stride < count:
        value = value + lax.ppermute(value, axis, [(i, i ^ stride) for i in range(count)])
        stride *= 2
    return value


def exchange(edge):
    head, tail, first, last = edge
    ring = lax.axis_size("space")
    line = lax.axis_size("tm")
    left = lax.ppermute(tail, "space", [(i, (i + 1) % ring) for i in range(ring)])
    right = lax.ppermute(head, "space", [((i + 1) % ring, i) for i in range(ring)])
    before = lax.ppermute(last, "tm", [(i, i + 1) for i in range(line - 1)])
    after = lax.ppermute(first, "tm", [(i + 1, i) for i in range(line - 1)])
    return left, right, before, after


def body(start_block, stiffness_tiles, tile_columns):
    slices, width, local_points = start_block.shape
    local_blocks = local_points // TILE
    first_block = lax.axis_index("space") * local_blocks
    blocks_all = lax.axis_size("space") * local_blocks
    place = (tile_columns - first_block + HB) % blocks_all
    count_all = slices * local_points * lax.axis_size("tm") * lax.axis_size("space")
    slice_index = lax.axis_index("tm") * slices + jnp.arange(slices, dtype=jnp.int32)
    last_slice = lax.axis_size("tm") * slices - 1
    degree = 2.0 - (slice_index == 0).astype(F32) - (slice_index == last_slice).astype(F32)

    y, *edge = start(start_block)
    tiles = prep(stiffness_tiles)

    def apply(mode, scale, y, edge, previous=None, matrix=None):
        halo = exchange(edge)
        part = local_part(place, tiles, y)
        return finish(mode, scale, place, degree, tiles, part, y, halo, previous, matrix)

    def run_filter(y, edge, mode, matrix=None):
        y0 = y
        y1, *edge = apply("first", 1.0 / RADIUS, y0, edge)
        y2, *edge = apply("step", 2.0 / RADIUS, y1, edge, y0)
        out = apply(mode, 2.0 / RADIUS, y2, edge, y1, matrix() if matrix else None)
        return out[0], out[1:5], out[5]

    filtered, edge, gram = run_filter(y, edge, "gram")
    kept = {}

    def first_matrix():
        total = total_over(total_over(gram, "tm"), "space")
        kept["first"], matrix = orth(total, filtered, count_all)
        return matrix

    second, edge, gram_two = run_filter(filtered, edge, "mixed", first_matrix)
    (product,) = apply("image", 1.0, second, edge)
    ritz_basis, matrix = orth(total_over(total_over(gram_two, "tm"), "space"), second, count_all)
    product = total_over(total_over(product, "tm"), "space")
    return ritz_basis, kept["first"], ritz(matrix, product, count_all)


def solution(mesh):
    placed = (P("tm", None, "space"), P("tm", "space", None, None), P("tm", "space"))
    return jax.shard_map(
        body,
        mesh=mesh,
        in_specs=placed,
        out_specs=(P("tm", None, "space"), P("tm", None, "space"), P()),
        check_vma=False,
    )
```

```python
import functools

import jax
import jax.numpy as jnp
from jax import lax
from jax.experimental import pallas as pl
from jax.experimental.pallas import tpu as pltpu
from jax.sharding import PartitionSpec as P

TILE = 128
TPR = 5
HB = 8
CENTER = 6.5
RADIUS = 3.5
INFLATION_FACTOR = 0.8

F32 = jnp.float32
BF16 = jnp.bfloat16
VM = pltpu.VMEM
NT = (((1,), (1,)), ((), ()))
NN = (((1,), (0,)), ((), ()))
WHOLE = pl.BlockSpec(memory_space=VM)
SCALARS = pl.BlockSpec(memory_space=pltpu.SMEM)


def near(x):
    return pltpu.with_memory_space_constraint(x, VM)


def split(x):
    high = x.astype(BF16)
    return high, (x - high.astype(F32)).astype(BF16)


def stacked(x):
    return jnp.concatenate(split(x), axis=0)


def call(kernel, ins, outs, scratch=(), specs=None, flops=0, moved=0, name=None, out_vmem=True):
    out_shape = [VM(s, d) if out_vmem else jax.ShapeDtypeStruct(s, d) for s, d in outs]
    return pl.pallas_call(
        kernel,
        out_shape=out_shape,
        in_specs=specs,
        out_specs=[WHOLE] * len(outs),
        scratch_shapes=list(scratch),
        name=name,
        cost_estimate=pl.CostEstimate(flops=flops, bytes_accessed=moved, transcendentals=0),
        compiler_params=pltpu.CompilerParams(vmem_limit_bytes=6 << 20),
    )(*ins)


def prep_kernel(tiles_ref, out_ref):
    for r in range(out_ref.shape[1]):
        for n in range(TPR):
            high, low = split(tiles_ref[0, r * TPR + n])
            out_ref[0, r, :TILE, n * TILE : (n + 1) * TILE] = high
            out_ref[0, r, TILE:, n * TILE : (n + 1) * TILE] = low


def prep(tiles):
    slices, count = tiles.shape[:2]
    rows = count // TPR
    step = 4
    return pl.pallas_call(
        prep_kernel,
        grid=(slices, rows // step),
        out_shape=VM((slices, rows, 2 * TILE, TPR * TILE), BF16),
        in_specs=[pl.BlockSpec((1, step * TPR, TILE, TILE), lambda s, i: (s, i, 0, 0))],
        out_specs=pl.BlockSpec((1, step, 2 * TILE, TPR * TILE), lambda s, i: (s, i, 0, 0)),
        name="prep",
        cost_estimate=pl.CostEstimate(
            flops=0, bytes_accessed=2 * 4 * tiles.size, transcendentals=0
        ),
        compiler_params=pltpu.CompilerParams(vmem_limit_bytes=8 << 20),
    )(tiles)


def edges(odd_ref, y_ref, inner_ref, outer_ref, near_ref, far_ref):
    width = HB * TILE
    points = y_ref.shape[2]
    final = y_ref.shape[0] - 1
    head = lambda: y_ref[:, :, :width]
    tail = lambda: y_ref[:, :, points - width :]
    first = lambda: y_ref[:1]
    last = lambda: y_ref[final:]
    for axis, inner, outer, low, high in (
        (0, inner_ref, outer_ref, head, tail),
        (1, near_ref, far_ref, first, last),
    ):

        @pl.when(odd_ref[axis] == 0)
        def _(inner=inner, outer=outer, low=low, high=high):
            inner[...] = high()
            outer[...] = low()

        @pl.when(odd_ref[axis] != 0)
        def _(inner=inner, outer=outer, low=low, high=high):
            inner[...] = low()
            outer[...] = high()


def edge_shapes(shape):
    slices, width, points = shape
    side = (slices, width, HB * TILE)
    return [(shape, F32), (side, F32), (side, F32), ((1, width, points), F32), ((1, width, points), F32)]


def start_kernel(odd_ref, x_ref, y_ref, *edge_refs):
    y_ref[...] = x_ref[...]
    edges(odd_ref, y_ref, *edge_refs)


def start(odd, block):
    return call(
        start_kernel,
        [odd, block],
        edge_shapes(block.shape),
        specs=[SCALARS, WHOLE],
        moved=16 * block.size,
        name="start",
    )


def fold(product, width):
    return product[:width, :TILE] + product[:width, TILE:] + product[width:, :TILE]


def row_product(halves_ref, places, tiles, width):
    left = jnp.concatenate([halves_ref[where] for where in places], axis=1)
    return fold(lax.dot_general(left, tiles, NT, preferred_element_type=F32), width)


def local_kernel(place_ref, tiles_ref, y_ref, out_ref, halves_ref):
    slices, width, points = y_ref.shape
    blocks = points // TILE
    for s in range(slices):
        for b in range(blocks):
            halves_ref[s * blocks + b] = stacked(y_ref[s, :, b * TILE : (b + 1) * TILE])
    halves_ref[slices * blocks] = jnp.zeros((2 * width, TILE), BF16)

    def row(i, carry):
        s, r = i // blocks, i % blocks
        places = []
        for n in range(TPR):
            where = place_ref[s, r * TPR + n] - HB
            inside = jnp.logical_and(where >= 0, where < blocks)
            places.append(jnp.where(inside, s * blocks + where, slices * blocks))
        here = pl.ds(pl.multiple_of(r * TILE, TILE), TILE)
        out_ref[s, :, here] = row_product(halves_ref, places, tiles_ref[s, r], width)
        return carry

    lax.fori_loop(0, slices * blocks, row, 0, unroll=4)


def local_part(place, tiles, y):
    slices, width, points = y.shape
    blocks = points // TILE
    return call(
        local_kernel,
        [place, near(tiles), near(y)],
        [(y.shape, F32)],
        specs=[SCALARS, WHOLE, WHOLE],
        scratch=[VM((slices * blocks + 1, 2 * width, TILE), BF16)],
        flops=2 * slices * blocks * TPR * 4 * width * TILE * TILE,
        moved=8 * y.size,
        name="local",
    )[0]


def mix(matrix, y):
    high, low = split(matrix)
    y_high, y_low = split(y)
    left = jnp.concatenate([high, low, high], axis=1)
    right = jnp.concatenate([y_high, y_high, y_low], axis=0)
    return lax.dot_general(left, right, NN, preferred_element_type=F32)


def inner(left, right):
    width = left.shape[0]
    p = lax.dot_general(stacked(left), stacked(right), NT, preferred_element_type=F32)
    return (p[:width, :width] + p[width:, width:]) + (p[:width, width:] + p[width:, :width])


def finish_kernel(mode, scale, *refs):
    refs = list(refs)
    take = lambda n: [refs.pop(0) for _ in range(n)]
    place_ref, odd_ref, tiles_ref, part_ref, y_ref = take(5)
    inner_ref, outer_ref, near_ref, far_ref = take(4)
    previous_ref = take(1)[0] if mode in ("step", "gram", "mixed") else None
    matrix_ref = take(1)[0] if mode == "mixed" else None
    if mode == "image":
        (gram_ref,) = take(1)
    else:
        new_ref, *edge_refs = take(5)
        gram_ref = take(1)[0] if mode in ("gram", "mixed") else None
    halves_ref = take(1)[0]
    if mode == "image":
        new_ref = take(1)[0]
    slices, width, points = y_ref.shape
    blocks = points // TILE
    for s in range(slices):
        for b in range(HB):
            at = s * 2 * HB + b
            halves_ref[at] = stacked(inner_ref[s, :, b * TILE : (b + 1) * TILE])
            halves_ref[at + HB] = stacked(outer_ref[s, :, b * TILE : (b + 1) * TILE])
    zero = slices * 2 * HB
    halves_ref[zero] = jnp.zeros((2 * width, TILE), BF16)
    left_at = jnp.where(odd_ref[0] == 0, HB, 0)
    right_at = HB - left_at - HB - blocks
    time_odd = odd_ref[1] != 0
    opening = odd_ref[2] != 0
    closing = odd_ref[3] != 0

    for s in range(slices):
        degree = 2.0
        if s == 0:
            degree = degree - jnp.where(opening, 1.0, 0.0)
        if s == slices - 1:
            degree = degree - jnp.where(closing, 1.0, 0.0)

        def row(r, carry, s=s, degree=degree):
            places = []
            for n in range(1, TPR):
                where = place_ref[s, r * TPR + n]
                right = where >= HB + blocks
                left = where < HB
                at = s * 2 * HB + where + jnp.where(right, right_at, left_at)
                places.append(jnp.where(jnp.logical_or(left, right), at, zero))
            product = row_product(halves_ref, places, tiles_ref[s, r, :, TILE:], width)
            here = pl.ds(pl.multiple_of(r * TILE, TILE), TILE)
            y = y_ref[s, :, here]
            if s == 0:
                before = jnp.where(time_odd, near_ref[0, :, here], far_ref[0, :, here])
                before = jnp.where(opening, 0.0, before)
            else:
                before = y_ref[s - 1, :, here]
            if s == slices - 1:
                after = jnp.where(time_odd, far_ref[0, :, here], near_ref[0, :, here])
                after = jnp.where(closing, 0.0, after)
            else:
                after = y_ref[s + 1, :, here]
            image = part_ref[s, :, here] + product
            image = image + INFLATION_FACTOR * (degree * y - before - after)
            if mode != "image":
                image = (image - CENTER * y) * scale
                if previous_ref is not None:
                    image = image - previous_ref[s, :, here]
            new_ref[s, :, here] = image
            return carry

        lax.fori_loop(0, blocks, row, 0, unroll=4)

    if mode == "mixed":
        for s in range(slices):
            new_ref[s] = mix(matrix_ref[...], new_ref[s])
    if mode != "image":
        edges(odd_ref, new_ref, *edge_refs)
    if gram_ref is not None:
        base_ref = y_ref if mode == "image" else new_ref
        total = inner(base_ref[0], new_ref[0])
        for s in range(1, slices):
            total = total + inner(base_ref[s], new_ref[s])
        gram_ref[...] = total


def finish(mode, scale, place, odd, tiles, part, y, halo, previous=None, matrix=None):
    slices, width, points = y.shape
    blocks = points // TILE
    ins = [place, odd] + [near(v) for v in (tiles, part, y, *halo)]
    specs = [SCALARS, SCALARS] + [WHOLE] * 7
    for extra in (previous, matrix):
        if extra is not None:
            ins.append(near(extra))
            specs.append(WHOLE)
    outs = [] if mode == "image" else edge_shapes(y.shape)
    if mode in ("gram", "mixed", "image"):
        outs = outs + [((width, width), F32)]
    scratch = [VM((slices * 2 * HB + 1, 2 * width, TILE), BF16)]
    if mode == "image":
        scratch.append(VM(y.shape, F32))
    return call(
        functools.partial(finish_kernel, mode, scale),
        ins,
        outs,
        scratch=scratch,
        specs=specs,
        flops=2 * slices * blocks * TPR * 4 * width * TILE * TILE,
        moved=24 * y.size,
        name="finish_" + mode,
    )


def inverse_factor(gram):
    width = gram.shape[0]
    rows = lax.broadcasted_iota(jnp.int32, (width, width), 0)
    columns = lax.broadcasted_iota(jnp.int32, (width, width), 1)
    inverse = (rows == columns).astype(F32)
    row_of = lax.broadcasted_iota(jnp.int32, (width, 1), 0)
    for j in range(width):
        root = lax.rsqrt(gram[j : j + 1, j : j + 1])
        gram_row = gram[j : j + 1, :] * root
        inverse_row = inverse[j : j + 1, :] * root
        column = jnp.where(row_of > j, gram[:, j : j + 1] * root, 0.0)
        gram = gram - column * gram_row
        inverse = jnp.where(row_of == j, inverse_row, inverse - column * inverse_row)
    return inverse


def orth_kernel(count, gram_ref, y_ref, out_ref, matrix_ref):
    matrix = inverse_factor(gram_ref[...] * (1.0 / count))
    matrix_ref[...] = matrix
    for s in range(y_ref.shape[0]):
        out_ref[s] = mix(matrix, y_ref[s])


def orth(gram, y, count):
    width = gram.shape[0]
    return pl.pallas_call(
        functools.partial(orth_kernel, float(count)),
        out_shape=[jax.ShapeDtypeStruct(y.shape, F32), VM((width, width), F32)],
        in_specs=[WHOLE, WHOLE],
        out_specs=[WHOLE, WHOLE],
        name="orth",
        cost_estimate=pl.CostEstimate(flops=2 * width * y.size, bytes_accessed=8 * y.size, transcendentals=0),
        compiler_params=pltpu.CompilerParams(vmem_limit_bytes=6 << 20),
    )(near(gram), near(y))


def ritz_kernel(count, matrix_ref, inner_ref, out_ref):
    high = lax.Precision.HIGHEST
    matrix = matrix_ref[...]
    half = lax.dot_general(matrix, inner_ref[...] * (1.0 / count), NN, precision=high, preferred_element_type=F32)
    out_ref[...] = lax.dot_general(half, matrix, NT, precision=high, preferred_element_type=F32)


def ritz(matrix, product, count):
    return call(
        functools.partial(ritz_kernel, float(count)),
        [near(matrix), near(product)],
        [(product.shape, F32)],
        specs=[WHOLE, WHOLE],
        name="ritz",
        moved=4 * product.size,
        out_vmem=False,
    )[0]


def total_over(value, axis):
    count = lax.axis_size(axis)
    stride = 1
    while stride < count:
        value = value + lax.ppermute(value, axis, [(i, i ^ stride) for i in range(count)])
        stride *= 2
    return value


def inner_pairs(axis):
    count = lax.axis_size(axis)
    return [(i, i ^ 1) for i in range(count)]


def outer_pairs(axis):
    count = lax.axis_size(axis)
    return [(i, (i + 1) % count if i % 2 else (i - 1) % count) for i in range(count)]


def exchange(edge):
    inner, outer, near_slice, far_slice = edge
    inner = lax.ppermute(inner, "space", inner_pairs("space"))
    outer = lax.ppermute(outer, "space", outer_pairs("space"))
    far_slice = lax.ppermute(far_slice, "tm", outer_pairs("tm"))
    near_slice = lax.ppermute(near_slice, "tm", inner_pairs("tm"))
    return inner, outer, near_slice, far_slice


def body(start_block, stiffness_tiles, tile_columns):
    slices, width, local_points = start_block.shape
    local_blocks = local_points // TILE
    first_block = lax.axis_index("space") * local_blocks
    blocks_all = lax.axis_size("space") * local_blocks
    place = (tile_columns - first_block + HB) % blocks_all
    count_all = slices * local_points * lax.axis_size("tm") * lax.axis_size("space")
    time_index = lax.axis_index("tm")
    ends = (time_index == 0, time_index == lax.axis_size("tm") - 1)
    odd = jnp.stack(
        [lax.axis_index("space") % 2, time_index % 2, ends[0].astype(jnp.int32), ends[1].astype(jnp.int32)]
    )

    y, *edge = start(odd, start_block)
    tiles = prep(stiffness_tiles)

    def apply(mode, scale, y, edge, previous=None, matrix=None):
        halo = exchange(edge)
        part = local_part(place, tiles, y)
        return finish(mode, scale, place, odd, tiles, part, y, halo, previous, matrix)

    def run_filter(y, edge, mode, matrix=None):
        y0 = y
        y1, *edge = apply("first", 1.0 / RADIUS, y0, edge)
        y2, *edge = apply("step", 2.0 / RADIUS, y1, edge, y0)
        out = apply(mode, 2.0 / RADIUS, y2, edge, y1, matrix() if matrix else None)
        return out[0], out[1:5], out[5]

    filtered, edge, gram = run_filter(y, edge, "gram")
    kept = {}

    def first_matrix():
        total = total_over(total_over(gram, "tm"), "space")
        kept["first"], matrix = orth(total, filtered, count_all)
        return matrix

    second, edge, gram_two = run_filter(filtered, edge, "mixed", first_matrix)
    (product,) = apply("image", 1.0, second, edge)
    ritz_basis, matrix = orth(total_over(total_over(gram_two, "tm"), "space"), second, count_all)
    product = total_over(total_over(product, "tm"), "space")
    return ritz_basis, kept["first"], ritz(matrix, product, count_all)


def solution(mesh):
    placed = (P("tm", None, "space"), P("tm", "space", None, None), P("tm", "space"))
    return jax.shard_map(
        body,
        mesh=mesh,
        in_specs=placed,
        out_specs=(P("tm", None, "space"), P("tm", None, "space"), P()),
        check_vma=False,
    )
```

```python
import functools

import jax
import jax.numpy as jnp
from jax import lax
from jax.experimental import pallas as pl
from jax.experimental.pallas import tpu as pltpu
from jax.sharding import PartitionSpec as P

TILE = 128
TPR = 5
HB = 8
CENTER = 6.5
RADIUS = 3.5
INFLATION_FACTOR = 0.8
GROUP = 8

F32 = jnp.float32
BF16 = jnp.bfloat16
VM = pltpu.VMEM
NT = (((1,), (1,)), ((), ()))
NN = (((1,), (0,)), ((), ()))
WHOLE = pl.BlockSpec(memory_space=VM)
SCALARS = pl.BlockSpec(memory_space=pltpu.SMEM)


def near(x):
    return pltpu.with_memory_space_constraint(x, VM)


def split(x):
    high = x.astype(BF16)
    return high, (x - high.astype(F32)).astype(BF16)


def stacked(x):
    return jnp.concatenate(split(x), axis=0)


def call(kernel, ins, outs, scratch=(), specs=None, flops=0, moved=0, name=None, out_vmem=True):
    out_shape = [VM(s, d) if out_vmem else jax.ShapeDtypeStruct(s, d) for s, d in outs]
    return pl.pallas_call(
        kernel,
        out_shape=out_shape,
        in_specs=specs,
        out_specs=[WHOLE] * len(outs),
        scratch_shapes=list(scratch),
        name=name,
        cost_estimate=pl.CostEstimate(flops=flops, bytes_accessed=moved, transcendentals=0),
        compiler_params=pltpu.CompilerParams(vmem_limit_bytes=6 << 20),
    )(*ins)


def prep_kernel(tiles_ref, out_ref, buffer_ref, semaphores):
    slots, step = buffer_ref.shape[:2]
    chunks = tiles_ref.shape[0] // step

    def copy(c):
        slot = lax.rem(c, slots)
        return pltpu.make_async_copy(
            tiles_ref.at[pl.ds(c * step, step)], buffer_ref.at[slot], semaphores.at[slot]
        )

    for c in range(slots):
        copy(c).start()

    def chunk(c, carry):
        copy(c).wait()
        slot = lax.rem(c, slots)
        for n in range(step):
            high, low = split(buffer_ref[slot, n].T)
            out_ref[c * step + n, :, :TILE] = high
            out_ref[c * step + n, :, TILE:] = low

        @pl.when(c + slots < chunks)
        def _():
            copy(c + slots).start()

        return carry

    lax.fori_loop(0, chunks, chunk, 0)


def prep(tiles):
    tiles = tiles.reshape(-1, TILE, TILE)
    slots, step = 5, 16
    return pl.pallas_call(
        prep_kernel,
        out_shape=VM((tiles.shape[0], TILE, 2 * TILE), BF16),
        in_specs=[pl.BlockSpec(memory_space=pltpu.HBM)],
        out_specs=WHOLE,
        scratch_shapes=[VM((slots, step, TILE, TILE), F32), pltpu.SemaphoreType.DMA((slots,))],
        name="prep",
        cost_estimate=pl.CostEstimate(flops=0, bytes_accessed=4 * tiles.size, transcendentals=0),
        compiler_params=pltpu.CompilerParams(vmem_limit_bytes=8 << 20),
    )(pltpu.with_memory_space_constraint(tiles, pltpu.HBM))


class Layout:
    def __init__(self, slices, blocks):
        most = slices * blocks * ((TPR - 1 + 1) // 2)
        room = most + GROUP + 2
        self.rows = slices * blocks * TPR
        self.tiles = self.rows + room
        self.places = self.tiles + 2 * room
        self.groups = self.places + 2 * room
        self.flags = self.groups + 1
        self.size = -(-(self.flags + 4) // 128) * 128


def plan_kernel(blocks_all, columns_ref, flags_ref, out_ref):
    slices, count = columns_ref.shape
    blocks = count // TPR
    at = Layout(slices, blocks)
    for i in range(4):
        out_ref[at.flags + i] = flags_ref[i]
    first_block = flags_ref[4]
    left_at = jnp.where(flags_ref[0] == 0, HB, 0)
    right_at = -left_at - blocks
    here = slices * blocks
    zero = slices * 2 * HB

    def row(i, units):
        s, r = i // blocks, i % blocks
        out_ref[at.rows + units] = i
        out_ref[at.rows + units + 1] = i
        found = jnp.int32(0)
        for n in range(TPR):
            where = columns_ref[s, r * TPR + n] - first_block + HB
            where = jnp.where(where < 0, where + blocks_all, where)
            where = jnp.where(where >= blocks_all, where - blocks_all, where)
            left = where < HB
            right = where >= HB + blocks
            away = jnp.logical_or(left, right)
            out_ref[i * TPR + n] = jnp.where(away, here, s * blocks + where - HB)
            if n > 0:
                out_ref[at.tiles + 2 * units + found] = i * TPR + n
                out_ref[at.places + 2 * units + found] = (
                    s * 2 * HB + where + jnp.where(right, right_at, left_at)
                )
                found = found + away.astype(jnp.int32)
        out_ref[at.tiles + 2 * units + found] = i * TPR
        out_ref[at.places + 2 * units + found] = zero
        return units + (found + 1) // 2

    units = lax.fori_loop(0, slices * blocks, row, jnp.int32(0))
    for n in range(GROUP):
        out_ref[at.rows + units + n] = 0
        for k in range(2):
            out_ref[at.tiles + 2 * (units + n) + k] = 0
            out_ref[at.places + 2 * (units + n) + k] = zero
    out_ref[at.groups] = (units + GROUP - 1) // GROUP


def plan(columns, flags, blocks_all):
    slices, count = columns.shape
    size = Layout(slices, count // TPR).size
    return pl.pallas_call(
        functools.partial(plan_kernel, blocks_all),
        out_shape=jax.ShapeDtypeStruct((size,), jnp.int32),
        in_specs=[SCALARS, SCALARS],
        out_specs=SCALARS,
        name="plan",
        compiler_params=pltpu.CompilerParams(vmem_limit_bytes=1 << 20),
    )(columns, flags)


def edges(flags, y_ref, inner_ref, outer_ref, near_ref, far_ref):
    width = HB * TILE
    points = y_ref.shape[2]
    final = y_ref.shape[0] - 1
    head = lambda: y_ref[:, :, :width]
    tail = lambda: y_ref[:, :, points - width :]
    first = lambda: y_ref[:1]
    last = lambda: y_ref[final:]
    for axis, inner, outer, low, high in (
        (0, inner_ref, outer_ref, head, tail),
        (1, near_ref, far_ref, first, last),
    ):

        @pl.when(flags[axis] == 0)
        def _(inner=inner, outer=outer, low=low, high=high):
            inner[...] = high()
            outer[...] = low()

        @pl.when(flags[axis] != 0)
        def _(inner=inner, outer=outer, low=low, high=high):
            inner[...] = low()
            outer[...] = high()


def edge_shapes(shape):
    slices, width, points = shape
    side = (slices, width, HB * TILE)
    return [(shape, F32), (side, F32), (side, F32), ((1, width, points), F32), ((1, width, points), F32)]


def start_kernel(odd_ref, x_ref, y_ref, *edge_refs):
    y_ref[...] = x_ref[...]
    edges([odd_ref[0], odd_ref[1]], y_ref, *edge_refs)


def start(odd, block):
    return call(
        start_kernel,
        [odd, block],
        edge_shapes(block.shape),
        specs=[SCALARS, WHOLE],
        moved=16 * block.size,
        name="start",
    )


def fold(product, width):
    return product[:width, :TILE] + product[:width, TILE:] + product[width:, :TILE]


def product(halves, tiles, width):
    left = jnp.concatenate(halves, axis=1)
    right = jnp.concatenate(tiles, axis=0)
    return fold(lax.dot_general(left, right, NN, preferred_element_type=F32), width)


def local_kernel(mode, scale, plan_ref, tiles_ref, y_ref, *refs):
    if mode in ("step", "gram", "mixed"):
        previous_ref, out_ref, halves_ref = refs
    else:
        previous_ref, (out_ref, halves_ref) = None, refs
    slices, width, points = y_ref.shape
    blocks = points // TILE
    at = Layout(slices, blocks)
    for s in range(slices):
        for b in range(blocks):
            halves_ref[s * blocks + b] = stacked(y_ref[s, :, b * TILE : (b + 1) * TILE])
    halves_ref[slices * blocks] = jnp.zeros((2 * width, TILE), BF16)

    for s in range(slices):
        degree = 2.0
        if s == 0:
            degree = degree - jnp.where(plan_ref[at.flags + 2] != 0, 1.0, 0.0)
        if s == slices - 1:
            degree = degree - jnp.where(plan_ref[at.flags + 3] != 0, 1.0, 0.0)

        def row(r, carry, s=s, degree=degree):
            i = s * blocks + r
            halves = [halves_ref[plan_ref[i * TPR + n]] for n in range(TPR)]
            tiles = [tiles_ref[i * TPR + n] for n in range(TPR)]
            here = pl.ds(pl.multiple_of(r * TILE, TILE), TILE)
            y = y_ref[s, :, here]
            time = degree * y
            if s > 0:
                time = time - y_ref[s - 1, :, here]
            if s < slices - 1:
                time = time - y_ref[s + 1, :, here]
            image = product(halves, tiles, width) + INFLATION_FACTOR * time
            if mode != "image":
                image = (image - CENTER * y) * scale
            if previous_ref is not None:
                image = image - previous_ref[s, :, here]
            out_ref[s, :, here] = image
            return carry

        lax.fori_loop(0, blocks, row, 0, unroll=8)


def local_part(mode, scale, table, tiles, y, previous):
    slices, width, points = y.shape
    blocks = points // TILE
    ins = [table, near(tiles), near(y)] + ([] if previous is None else [near(previous)])
    return call(
        functools.partial(local_kernel, mode, scale),
        ins,
        [(y.shape, F32)],
        specs=[SCALARS] + [WHOLE] * (len(ins) - 1),
        scratch=[VM((slices * blocks + 1, 2 * width, TILE), BF16)],
        flops=2 * slices * blocks * TPR * 4 * width * TILE * TILE,
        moved=12 * y.size,
        name="local_" + mode,
    )[0]


def mix(matrix, y):
    high, low = split(matrix)
    y_high, y_low = split(y)
    left = jnp.concatenate([high, low, high], axis=1)
    right = jnp.concatenate([y_high, y_high, y_low], axis=0)
    return lax.dot_general(left, right, NN, preferred_element_type=F32)


def inner(left, right):
    width = left.shape[0]
    p = lax.dot_general(stacked(left), stacked(right), NT, preferred_element_type=F32)
    return (p[:width, :width] + p[width:, width:]) + (p[:width, width:] + p[width:, :width])


def finish_kernel(mode, scale, *refs):
    refs = list(refs)
    take = lambda n: [refs.pop(0) for _ in range(n)]
    plan_ref, tiles_ref, part_ref = take(3)
    inner_ref, outer_ref, near_ref, far_ref = take(4)
    y_ref = take(1)[0] if mode == "image" else None
    matrix_ref = take(1)[0] if mode == "mixed" else None
    if mode == "image":
        gram_ref, halves_ref, new_ref = refs
    else:
        new_ref, *edge_refs = take(5)
        gram_ref = take(1)[0] if mode in ("gram", "mixed") else None
        (halves_ref,) = refs
    slices, width, points = part_ref.shape
    blocks = points // TILE
    at = Layout(slices, blocks)
    for s in range(slices):
        for b in range(HB):
            to = s * 2 * HB + b
            halves_ref[to] = stacked(inner_ref[s, :, b * TILE : (b + 1) * TILE])
            halves_ref[to + HB] = stacked(outer_ref[s, :, b * TILE : (b + 1) * TILE])
    halves_ref[slices * 2 * HB] = jnp.zeros((2 * width, TILE), BF16)

    time_odd = plan_ref[at.flags + 1] != 0
    factor = INFLATION_FACTOR * scale
    for s in range(slices):
        image = part_ref[s]
        if s == 0:
            before = jnp.where(time_odd, near_ref[0], far_ref[0])
            image = image - jnp.where(plan_ref[at.flags + 2] != 0, 0.0, factor * before)
        if s == slices - 1:
            after = jnp.where(time_odd, far_ref[0], near_ref[0])
            image = image - jnp.where(plan_ref[at.flags + 3] != 0, 0.0, factor * after)
        new_ref[s] = image

    def group(g, carry):
        done = []
        for k in range(GROUP):
            u = g * GROUP + k
            halves = [halves_ref[plan_ref[at.places + 2 * u + j]] for j in range(2)]
            tiles = [plan_ref[at.tiles + 2 * u + j] for j in range(2)]
            tiles = [tiles_ref[t] for t in tiles]
            done.append((plan_ref[at.rows + u], product(halves, tiles, width)))
        for i, value in done:
            here = pl.ds(pl.multiple_of((i % blocks) * TILE, TILE), TILE)
            new_ref[i // blocks, :, here] += scale * value
        return carry

    lax.fori_loop(0, plan_ref[at.groups], group, 0)

    if mode == "mixed":
        for s in range(slices):
            new_ref[s] = mix(matrix_ref[...], new_ref[s])
    if mode != "image":
        edges([plan_ref[at.flags], plan_ref[at.flags + 1]], new_ref, *edge_refs)
    if gram_ref is not None:
        base_ref = y_ref if mode == "image" else new_ref
        total = inner(base_ref[0], new_ref[0])
        for s in range(1, slices):
            total = total + inner(base_ref[s], new_ref[s])
        gram_ref[...] = total


def finish(mode, scale, table, tiles, part, y, halo, matrix=None):
    slices, width, points = y.shape
    blocks = points // TILE
    ins = [table] + [near(v) for v in (tiles, part, *halo)]
    if mode == "image":
        ins.append(near(y))
    if matrix is not None:
        ins.append(near(matrix))
    outs = [] if mode == "image" else edge_shapes(y.shape)
    if mode in ("gram", "mixed", "image"):
        outs = outs + [((width, width), F32)]
    scratch = [VM((slices * 2 * HB + 1, 2 * width, TILE), BF16)]
    if mode == "image":
        scratch.append(VM(y.shape, F32))
    return call(
        functools.partial(finish_kernel, mode, scale),
        ins,
        outs,
        scratch=scratch,
        specs=[SCALARS] + [WHOLE] * (len(ins) - 1),
        flops=2 * slices * blocks * 2 * 4 * width * TILE * TILE,
        moved=24 * y.size,
        name="finish_" + mode,
    )


def inverse_factor(gram):
    width = gram.shape[0]
    rows = lax.broadcasted_iota(jnp.int32, (width, width), 0)
    columns = lax.broadcasted_iota(jnp.int32, (width, width), 1)
    inverse = (rows == columns).astype(F32)
    row_of = lax.broadcasted_iota(jnp.int32, (width, 1), 0)
    for j in range(width):
        root = lax.rsqrt(gram[j : j + 1, j : j + 1])
        gram_row = gram[j : j + 1, :] * root
        inverse_row = inverse[j : j + 1, :] * root
        column = jnp.where(row_of > j, gram[:, j : j + 1] * root, 0.0)
        gram = gram - column * gram_row
        inverse = jnp.where(row_of == j, inverse_row, inverse - column * inverse_row)
    return inverse


def orth_kernel(count, gram_ref, y_ref, out_ref, matrix_ref):
    matrix = inverse_factor(gram_ref[...] * (1.0 / count))
    matrix_ref[...] = matrix
    for s in range(y_ref.shape[0]):
        out_ref[s] = mix(matrix, y_ref[s])


def orth(gram, y, count):
    width = gram.shape[0]
    return pl.pallas_call(
        functools.partial(orth_kernel, float(count)),
        out_shape=[jax.ShapeDtypeStruct(y.shape, F32), VM((width, width), F32)],
        in_specs=[WHOLE, WHOLE],
        out_specs=[WHOLE, WHOLE],
        name="orth",
        cost_estimate=pl.CostEstimate(flops=2 * width * y.size, bytes_accessed=8 * y.size, transcendentals=0),
        compiler_params=pltpu.CompilerParams(vmem_limit_bytes=6 << 20),
    )(near(gram), near(y))


def ritz_kernel(count, matrix_ref, inner_ref, out_ref):
    high = lax.Precision.HIGHEST
    matrix = matrix_ref[...]
    half = lax.dot_general(matrix, inner_ref[...] * (1.0 / count), NN, precision=high, preferred_element_type=F32)
    out_ref[...] = lax.dot_general(half, matrix, NT, precision=high, preferred_element_type=F32)


def ritz(matrix, product, count):
    return call(
        functools.partial(ritz_kernel, float(count)),
        [near(matrix), near(product)],
        [(product.shape, F32)],
        specs=[WHOLE, WHOLE],
        name="ritz",
        moved=4 * product.size,
        out_vmem=False,
    )[0]


def stages_of(axis):
    count = lax.axis_size(axis)
    found, stride = [], 1
    if (count.bit_length() - 1) % 2:
        found, stride = [(axis, (1,))], 2
    while stride < count:
        found.append((axis, (stride, 2 * stride, 3 * stride)))
        stride *= 4
    return found


def add_over(value, stages):
    for axis, strides in stages:
        count = lax.axis_size(axis)
        others = [lax.ppermute(value, axis, [(i, i ^ k) for i in range(count)]) for k in strides]
        if len(others) == 1:
            value = value + others[0]
        else:
            value = (value + others[0]) + (others[1] + others[2])
    return value


def inner_pairs(axis):
    count = lax.axis_size(axis)
    return [(i, i ^ 1) for i in range(count)]


def outer_pairs(axis):
    count = lax.axis_size(axis)
    return [(i, (i + 1) % count if i % 2 else (i - 1) % count) for i in range(count)]


def exchange(edge):
    inner, outer, near_slice, far_slice = edge
    inner = lax.ppermute(inner, "space", inner_pairs("space"))
    outer = lax.ppermute(outer, "space", outer_pairs("space"))
    far_slice = lax.ppermute(far_slice, "tm", outer_pairs("tm"))
    near_slice = lax.ppermute(near_slice, "tm", inner_pairs("tm"))
    return inner, outer, near_slice, far_slice


def body(start_block, stiffness_tiles, tile_columns):
    slices, width, local_points = start_block.shape
    local_blocks = local_points // TILE
    blocks_all = lax.axis_size("space") * local_blocks
    count_all = slices * local_points * lax.axis_size("tm") * lax.axis_size("space")
    time_index = lax.axis_index("tm")
    ends = (time_index == 0, time_index == lax.axis_size("tm") - 1)
    space_index = lax.axis_index("space")
    odd = jnp.stack(
        [
            space_index % 2,
            time_index % 2,
            ends[0].astype(jnp.int32),
            ends[1].astype(jnp.int32),
            space_index * local_blocks,
        ]
    )

    y, *edge = start(odd, start_block)
    table = plan(tile_columns, odd, blocks_all)
    tiles = prep(stiffness_tiles)

    across, along = stages_of("space"), stages_of("tm")
    early, late = across + along[::-1], along + across
    share = -(-len(early) // 3)

    def apply(mode, scale, y, edge, previous=None, beside=None):
        halo = exchange(edge)
        part = local_part(mode, scale, table, tiles, y, previous)
        extra = beside() if beside else None
        if extra is not None:
            part, extra = lax.optimization_barrier((part, extra))
        matrix = extra if mode == "mixed" else None
        return finish(mode, scale, table, tiles, part, y, halo, matrix), extra

    (y1, *edge), _ = apply("first", 1.0 / RADIUS, y, edge)
    (y2, *edge), _ = apply("step", 2.0 / RADIUS, y1, edge, y)
    (filtered, *edge, gram), _ = apply("gram", 2.0 / RADIUS, y2, edge, y1)

    kept = {}

    def first_matrix():
        total = add_over(gram, early[2 * share :])
        kept["first"], matrix = orth(total, filtered, count_all)
        return matrix

    (y1, *edge), gram = apply(
        "first", 1.0 / RADIUS, filtered, edge, beside=lambda: add_over(gram, early[:share])
    )
    (y2, *edge), gram = apply(
        "step", 2.0 / RADIUS, y1, edge, filtered, beside=lambda: add_over(gram, early[share : 2 * share])
    )
    (second, *edge, gram_two), _ = apply("mixed", 2.0 / RADIUS, y2, edge, y1, beside=first_matrix)
    (inner_two,), gram_two = apply(
        "image", 1.0, second, edge, beside=lambda: add_over(gram_two, along)
    )
    ritz_basis, matrix = orth(add_over(gram_two, across), second, count_all)
    return ritz_basis, kept["first"], ritz(matrix, add_over(inner_two, late), count_all)


def solution(mesh):
    placed = (P("tm", None, "space"), P("tm", "space", None, None), P("tm", "space"))
    return jax.shard_map(
        body,
        mesh=mesh,
        in_specs=placed,
        out_specs=(P("tm", None, "space"), P("tm", None, "space"), P()),
        check_vma=False,
    )
```

```python
import functools

import jax
import jax.numpy as jnp
from jax import lax
from jax.experimental import pallas as pl
from jax.experimental.pallas import tpu as pltpu
from jax.sharding import PartitionSpec as P

TILE = 128
TPR = 5
HB = 8
CENTER = 6.5
RADIUS = 3.5
INFLATION_FACTOR = 0.8
GROUP = 8

F32 = jnp.float32
BF16 = jnp.bfloat16
VM = pltpu.VMEM
NT = (((1,), (1,)), ((), ()))
NN = (((1,), (0,)), ((), ()))
WHOLE = pl.BlockSpec(memory_space=VM)
SCALARS = pl.BlockSpec(memory_space=pltpu.SMEM)


def near(x):
    return pltpu.with_memory_space_constraint(x, VM)


def split(x):
    high = x.astype(BF16)
    return high, (x - high.astype(F32)).astype(BF16)


def stacked(x):
    return jnp.concatenate(split(x), axis=0)


def call(kernel, ins, outs, scratch=(), specs=None, flops=0, moved=0, name=None, out_vmem=True):
    out_shape = [VM(s, d) if out_vmem else jax.ShapeDtypeStruct(s, d) for s, d in outs]
    return pl.pallas_call(
        kernel,
        out_shape=out_shape,
        in_specs=specs,
        out_specs=[WHOLE] * len(outs),
        scratch_shapes=list(scratch),
        name=name,
        cost_estimate=pl.CostEstimate(flops=flops, bytes_accessed=moved, transcendentals=0),
        compiler_params=pltpu.CompilerParams(vmem_limit_bytes=6 << 20),
    )(*ins)


def prep_kernel(tiles_ref, out_ref, buffer_ref, semaphores):
    slots, step = buffer_ref.shape[:2]
    chunks = tiles_ref.shape[0] // step

    def copy(c):
        slot = lax.rem(c, slots)
        return pltpu.make_async_copy(
            tiles_ref.at[pl.ds(c * step, step)], buffer_ref.at[slot], semaphores.at[slot]
        )

    for c in range(slots):
        copy(c).start()

    def chunk(c, carry):
        copy(c).wait()
        slot = lax.rem(c, slots)
        for n in range(step):
            high, low = split(buffer_ref[slot, n].T)
            out_ref[c * step + n, :, :TILE] = high
            out_ref[c * step + n, :, TILE:] = low

        @pl.when(c + slots < chunks)
        def _():
            copy(c + slots).start()

        return carry

    lax.fori_loop(0, chunks, chunk, 0)


def prep(tiles):
    tiles = tiles.reshape(-1, TILE, TILE)
    slots, step = 5, 16
    return pl.pallas_call(
        prep_kernel,
        out_shape=VM((tiles.shape[0], TILE, 2 * TILE), BF16),
        in_specs=[pl.BlockSpec(memory_space=pltpu.HBM)],
        out_specs=WHOLE,
        scratch_shapes=[VM((slots, step, TILE, TILE), F32), pltpu.SemaphoreType.DMA((slots,))],
        name="prep",
        cost_estimate=pl.CostEstimate(flops=0, bytes_accessed=4 * tiles.size, transcendentals=0),
        compiler_params=pltpu.CompilerParams(vmem_limit_bytes=8 << 20),
    )(pltpu.with_memory_space_constraint(tiles, pltpu.HBM))


class Layout:
    def __init__(self, slices, blocks):
        most = slices * blocks * ((TPR - 1 + 1) // 2)
        room = most + GROUP + 2
        self.rows = slices * blocks * TPR
        self.tiles = self.rows + room
        self.places = self.tiles + 2 * room
        self.groups = self.places + 2 * room
        self.flags = self.groups + 1
        self.size = -(-(self.flags + 4) // 128) * 128


def plan_kernel(blocks_all, columns_ref, flags_ref, out_ref):
    slices, count = columns_ref.shape
    blocks = count // TPR
    at = Layout(slices, blocks)
    for i in range(4):
        out_ref[at.flags + i] = flags_ref[i]
    first_block = flags_ref[4]
    left_at = jnp.where(flags_ref[0] == 0, HB, 0)
    right_at = -left_at - blocks
    here = slices * blocks
    zero = slices * 2 * HB

    def row(i, units):
        s, r = i // blocks, i % blocks
        out_ref[at.rows + units] = i
        out_ref[at.rows + units + 1] = i
        found = jnp.int32(0)
        for n in range(TPR):
            where = columns_ref[s, r * TPR + n] - first_block + HB
            where = jnp.where(where < 0, where + blocks_all, where)
            where = jnp.where(where >= blocks_all, where - blocks_all, where)
            left = where < HB
            right = where >= HB + blocks
            away = jnp.logical_or(left, right)
            out_ref[i * TPR + n] = jnp.where(away, here, s * blocks + where - HB)
            if n > 0:
                out_ref[at.tiles + 2 * units + found] = i * TPR + n
                out_ref[at.places + 2 * units + found] = (
                    s * 2 * HB + where + jnp.where(right, right_at, left_at)
                )
                found = found + away.astype(jnp.int32)
        out_ref[at.tiles + 2 * units + found] = i * TPR
        out_ref[at.places + 2 * units + found] = zero
        return units + (found + 1) // 2

    units = lax.fori_loop(0, slices * blocks, row, jnp.int32(0), unroll=4)
    for n in range(GROUP):
        out_ref[at.rows + units + n] = 0
        for k in range(2):
            out_ref[at.tiles + 2 * (units + n) + k] = 0
            out_ref[at.places + 2 * (units + n) + k] = zero
    out_ref[at.groups] = (units + GROUP - 1) // GROUP


def plan(columns, flags, blocks_all):
    slices, count = columns.shape
    size = Layout(slices, count // TPR).size
    return pl.pallas_call(
        functools.partial(plan_kernel, blocks_all),
        out_shape=jax.ShapeDtypeStruct((size,), jnp.int32),
        in_specs=[SCALARS, SCALARS],
        out_specs=SCALARS,
        name="plan",
        compiler_params=pltpu.CompilerParams(vmem_limit_bytes=1 << 20),
    )(columns, flags)


def edges(flags, y_ref, inner_ref, outer_ref, near_ref, far_ref):
    width = HB * TILE
    points = y_ref.shape[2]
    final = y_ref.shape[0] - 1
    head = lambda: y_ref[:, :, :width]
    tail = lambda: y_ref[:, :, points - width :]
    first = lambda: y_ref[:1]
    last = lambda: y_ref[final:]
    for axis, inner, outer, low, high in (
        (0, inner_ref, outer_ref, head, tail),
        (1, near_ref, far_ref, first, last),
    ):

        @pl.when(flags[axis] == 0)
        def _(inner=inner, outer=outer, low=low, high=high):
            inner[...] = high()
            outer[...] = low()

        @pl.when(flags[axis] != 0)
        def _(inner=inner, outer=outer, low=low, high=high):
            inner[...] = low()
            outer[...] = high()


def edge_shapes(shape):
    slices, width, points = shape
    side = (slices, width, HB * TILE)
    return [(shape, F32), (side, F32), (side, F32), ((1, width, points), F32), ((1, width, points), F32)]


def start_kernel(odd_ref, x_ref, y_ref, *edge_refs):
    y_ref[...] = x_ref[...]
    edges([odd_ref[0], odd_ref[1]], y_ref, *edge_refs)


def start(odd, block):
    return call(
        start_kernel,
        [odd, block],
        edge_shapes(block.shape),
        specs=[SCALARS, WHOLE],
        moved=16 * block.size,
        name="start",
    )


def fold(product, width):
    return product[:width, :TILE] + product[:width, TILE:] + product[width:, :TILE]


def product(halves, tiles, width):
    left = jnp.concatenate(halves, axis=1)
    right = jnp.concatenate(tiles, axis=0)
    return fold(lax.dot_general(left, right, NN, preferred_element_type=F32), width)


def local_kernel(mode, scale, plan_ref, tiles_ref, y_ref, *refs):
    if mode in ("step", "gram"):
        previous_ref, out_ref, halves_ref = refs
    else:
        previous_ref, (out_ref, halves_ref) = None, refs
    slices, width, points = y_ref.shape
    blocks = points // TILE
    at = Layout(slices, blocks)
    for s in range(slices):
        for b in range(blocks):
            halves_ref[s * blocks + b] = stacked(y_ref[s, :, b * TILE : (b + 1) * TILE])
    halves_ref[slices * blocks] = jnp.zeros((2 * width, TILE), BF16)

    for s in range(slices):
        degree = 2.0
        if s == 0:
            degree = degree - jnp.where(plan_ref[at.flags + 2] != 0, 1.0, 0.0)
        if s == slices - 1:
            degree = degree - jnp.where(plan_ref[at.flags + 3] != 0, 1.0, 0.0)

        def row(r, carry, s=s, degree=degree):
            i = s * blocks + r
            halves = [halves_ref[plan_ref[i * TPR + n]] for n in range(TPR)]
            tiles = [tiles_ref[i * TPR + n] for n in range(TPR)]
            here = pl.ds(pl.multiple_of(r * TILE, TILE), TILE)
            y = y_ref[s, :, here]
            time = degree * y
            if s > 0:
                time = time - y_ref[s - 1, :, here]
            if s < slices - 1:
                time = time - y_ref[s + 1, :, here]
            image = product(halves, tiles, width) + INFLATION_FACTOR * time
            if mode != "image":
                image = (image - CENTER * y) * scale
            if previous_ref is not None:
                image = image - previous_ref[s, :, here]
            out_ref[s, :, here] = image
            return carry

        lax.fori_loop(0, blocks, row, 0, unroll=8)


def local_part(mode, scale, table, tiles, y, previous):
    slices, width, points = y.shape
    blocks = points // TILE
    ins = [table, near(tiles), near(y)] + ([] if previous is None else [near(previous)])
    return call(
        functools.partial(local_kernel, mode, scale),
        ins,
        [(y.shape, F32)],
        specs=[SCALARS] + [WHOLE] * (len(ins) - 1),
        scratch=[VM((slices * blocks + 1, 2 * width, TILE), BF16)],
        flops=2 * slices * blocks * TPR * 4 * width * TILE * TILE,
        moved=12 * y.size,
        name="local_" + mode,
    )[0]


def mix(matrix, y):
    high, low = split(matrix)
    y_high, y_low = split(y)
    left = jnp.concatenate([high, low, high], axis=1)
    right = jnp.concatenate([y_high, y_high, y_low], axis=0)
    return lax.dot_general(left, right, NN, preferred_element_type=F32)


def inner(left, right):
    width = left.shape[0]
    p = lax.dot_general(stacked(left), stacked(right), NT, preferred_element_type=F32)
    return (p[:width, :width] + p[width:, width:]) + (p[:width, width:] + p[width:, :width])


def finish_kernel(mode, scale, *refs):
    refs = list(refs)
    take = lambda n: [refs.pop(0) for _ in range(n)]
    plan_ref, tiles_ref, part_ref = take(3)
    inner_ref, outer_ref, near_ref, far_ref = take(4)
    if mode == "image":
        y_ref, matrix_ref, mixed_ref, gram_ref, halves_ref, new_ref = refs
    else:
        new_ref, *edge_refs = take(5)
        gram_ref = take(1)[0] if mode == "gram" else None
        (halves_ref,) = refs
    slices, width, points = part_ref.shape
    blocks = points // TILE
    at = Layout(slices, blocks)
    for s in range(slices):
        for b in range(HB):
            to = s * 2 * HB + b
            halves_ref[to] = stacked(inner_ref[s, :, b * TILE : (b + 1) * TILE])
            halves_ref[to + HB] = stacked(outer_ref[s, :, b * TILE : (b + 1) * TILE])
    halves_ref[slices * 2 * HB] = jnp.zeros((2 * width, TILE), BF16)

    time_odd = plan_ref[at.flags + 1] != 0
    factor = INFLATION_FACTOR * scale
    for s in range(slices):
        image = part_ref[s]
        if s == 0:
            before = jnp.where(time_odd, near_ref[0], far_ref[0])
            image = image - jnp.where(plan_ref[at.flags + 2] != 0, 0.0, factor * before)
        if s == slices - 1:
            after = jnp.where(time_odd, far_ref[0], near_ref[0])
            image = image - jnp.where(plan_ref[at.flags + 3] != 0, 0.0, factor * after)
        new_ref[s] = image

    def group(g, carry):
        done = []
        for k in range(GROUP):
            u = g * GROUP + k
            halves = [halves_ref[plan_ref[at.places + 2 * u + j]] for j in range(2)]
            tiles = [plan_ref[at.tiles + 2 * u + j] for j in range(2)]
            tiles = [tiles_ref[t] for t in tiles]
            done.append((plan_ref[at.rows + u], product(halves, tiles, width)))
        for i, value in done:
            here = pl.ds(pl.multiple_of((i % blocks) * TILE, TILE), TILE)
            new_ref[i // blocks, :, here] += scale * value
        return carry

    lax.fori_loop(0, plan_ref[at.groups], group, 0)

    if mode != "image":
        edges([plan_ref[at.flags], plan_ref[at.flags + 1]], new_ref, *edge_refs)
    if mode == "gram":
        gram_ref[...] = sum(inner(new_ref[s], new_ref[s]) for s in range(slices))
    if mode == "image":
        matrix = matrix_ref[...]
        first, second = 0.0, 0.0
        for s in range(slices):
            mixed = mix(matrix, y_ref[s])
            mixed_ref[s] = mixed
            first = first + inner(mixed, mixed)
            second = second + inner(mixed, mix(matrix, new_ref[s]))
        gram_ref[:width] = first
        gram_ref[width:] = second


def finish(mode, scale, table, tiles, part, y, halo, matrix=None):
    slices, width, points = y.shape
    blocks = points // TILE
    ins = [table] + [near(v) for v in (tiles, part, *halo)]
    if mode == "image":
        ins += [near(y), near(matrix)]
        outs = [(y.shape, F32), ((2 * width, width), F32)]
    else:
        outs = edge_shapes(y.shape)
    if mode == "gram":
        outs = outs + [((width, width), F32)]
    scratch = [VM((slices * 2 * HB + 1, 2 * width, TILE), BF16)]
    if mode == "image":
        scratch.append(VM(y.shape, F32))
    return call(
        functools.partial(finish_kernel, mode, scale),
        ins,
        outs,
        scratch=scratch,
        specs=[SCALARS] + [WHOLE] * (len(ins) - 1),
        flops=2 * slices * blocks * 2 * 4 * width * TILE * TILE,
        moved=24 * y.size,
        name="finish_" + mode,
    )


def inverse_factor(gram):
    width = gram.shape[0]
    rows = lax.broadcasted_iota(jnp.int32, (width, width), 0)
    columns = lax.broadcasted_iota(jnp.int32, (width, width), 1)
    inverse = (rows == columns).astype(F32)
    row_of = lax.broadcasted_iota(jnp.int32, (width, 1), 0)
    for j in range(width):
        root = lax.rsqrt(gram[j : j + 1, j : j + 1])
        gram_row = gram[j : j + 1, :] * root
        inverse_row = inverse[j : j + 1, :] * root
        column = jnp.where(row_of > j, gram[:, j : j + 1] * root, 0.0)
        gram = gram - column * gram_row
        inverse = jnp.where(row_of == j, inverse_row, inverse - column * inverse_row)
    return inverse


def factor_kernel(count, gram_ref, out_ref):
    out_ref[...] = inverse_factor(gram_ref[...] * (1.0 / count))


def factor(gram, count):
    return call(
        functools.partial(factor_kernel, float(count)),
        [near(gram)],
        [(gram.shape, F32)],
        specs=[WHOLE],
        flops=40000 * gram.size,
        moved=8 * gram.size,
        name="factor",
    )[0]


def basis_kernel(matrix_ref, y_ref, out_ref):
    for s in range(y_ref.shape[0]):
        out_ref[s] = mix(matrix_ref[...], y_ref[s])


def basis(matrix, y):
    return call(
        basis_kernel,
        [near(matrix), near(y)],
        [(y.shape, F32)],
        specs=[WHOLE] * 2,
        flops=2 * matrix.shape[0] * y.size,
        moved=8 * y.size,
        name="basis",
        out_vmem=False,
    )[0]


def close_kernel(count, sums_ref, y_ref, basis_ref, ritz_ref):
    high = lax.Precision.HIGHEST
    width = sums_ref.shape[1]
    matrix = inverse_factor(sums_ref[:width] * (1.0 / count))
    projected = sums_ref[width:] * (1.0 / count)
    for s in range(y_ref.shape[0]):
        basis_ref[s] = mix(matrix, y_ref[s])
    half = lax.dot_general(matrix, projected, NN, precision=high, preferred_element_type=F32)
    ritz_ref[...] = lax.dot_general(half, matrix, NT, precision=high, preferred_element_type=F32)


def close(sums, y, count):
    width = sums.shape[1]
    return call(
        functools.partial(close_kernel, float(count)),
        [near(sums), near(y)],
        [(y.shape, F32), ((width, width), F32)],
        specs=[WHOLE] * 2,
        flops=2 * width * y.size,
        moved=8 * y.size,
        name="close",
        out_vmem=False,
    )


def stages_of(axis):
    count = lax.axis_size(axis)
    found, stride = [], 1
    if (count.bit_length() - 1) % 2:
        found, stride = [(axis, (1,))], 2
    while stride < count:
        found.append((axis, (stride, 2 * stride, 3 * stride)))
        stride *= 4
    return found


def pairs_of(axis):
    return [(axis, (1 << k,)) for k in range((lax.axis_size(axis) - 1).bit_length())]


def add_over(value, stages):
    for axis, strides in stages:
        count = lax.axis_size(axis)
        others = [lax.ppermute(value, axis, [(i, i ^ k) for i in range(count)]) for k in strides]
        if len(others) == 1:
            value = value + others[0]
        else:
            value = (value + others[0]) + (others[1] + others[2])
    return value


def inner_pairs(axis):
    count = lax.axis_size(axis)
    return [(i, i ^ 1) for i in range(count)]


def outer_pairs(axis):
    count = lax.axis_size(axis)
    return [(i, (i + 1) % count if i % 2 else (i - 1) % count) for i in range(count)]


def exchange(edge):
    inner, outer, near_slice, far_slice = edge
    inner = lax.ppermute(inner, "space", inner_pairs("space"))
    outer = lax.ppermute(outer, "space", outer_pairs("space"))
    far_slice = lax.ppermute(far_slice, "tm", outer_pairs("tm"))
    near_slice = lax.ppermute(near_slice, "tm", inner_pairs("tm"))
    return inner, outer, near_slice, far_slice


def body(start_block, stiffness_tiles, tile_columns):
    slices, width, local_points = start_block.shape
    local_blocks = local_points // TILE
    blocks_all = lax.axis_size("space") * local_blocks
    count_all = slices * local_points * lax.axis_size("tm") * lax.axis_size("space")
    time_index = lax.axis_index("tm")
    ends = (time_index == 0, time_index == lax.axis_size("tm") - 1)
    space_index = lax.axis_index("space")
    odd = jnp.stack(
        [
            space_index % 2,
            time_index % 2,
            ends[0].astype(jnp.int32),
            ends[1].astype(jnp.int32),
            space_index * local_blocks,
        ]
    )

    y, *edge = start(odd, start_block)
    table = plan(tile_columns, odd, blocks_all)
    tiles = prep(stiffness_tiles)

    across, along = pairs_of("space"), pairs_of("tm")
    half = -(-len(across) // 2)
    early = [along[:1] + across[:half], across[half:], along[1:-1], along[-1:]]

    def apply(mode, scale, y, edge, previous=None, beside=None):
        halo = exchange(edge)
        part = local_part(mode, scale, table, tiles, y, previous)
        extra = None
        if beside is not None:
            part, extra = lax.optimization_barrier((part, beside[0]))
            part, extra = lax.optimization_barrier((part, beside[1](extra)))
        return finish(mode, scale, table, tiles, part, y, halo, extra), extra

    (y1, *edge), _ = apply("first", 1.0 / RADIUS, y, edge)
    (y2, *edge), _ = apply("step", 2.0 / RADIUS, y1, edge, y)
    (filtered, *edge, gram), _ = apply("gram", 2.0 / RADIUS, y2, edge, y1)

    def stage(n):
        return lambda gram: add_over(gram, early[n])

    (y1, *edge), gram = apply("first", 1.0 / RADIUS, filtered, edge, None, (gram, stage(0)))
    (y2, *edge), gram = apply("step", 2.0 / RADIUS, y1, edge, filtered, (gram, stage(1)))
    (y3, *edge), gram = apply("step", 2.0 / RADIUS, y2, edge, y1, (gram, stage(2)))
    (second, sums), matrix = apply(
        "image", 1.0, y3, edge, None, (gram, lambda gram: factor(stage(3)(gram), count_all))
    )
    first_basis = basis(matrix, filtered)
    sums = add_over(sums, stages_of("tm") + stages_of("space"))
    ritz_basis, ritz_matrix = close(sums, second, count_all)
    return ritz_basis, first_basis, ritz_matrix


def solution(mesh):
    placed = (P("tm", None, "space"), P("tm", "space", None, None), P("tm", "space"))
    return jax.shard_map(
        body,
        mesh=mesh,
        in_specs=placed,
        out_specs=(P("tm", None, "space"), P("tm", None, "space"), P()),
        check_vma=False,
    )
```

```python
import functools

import jax
import jax.numpy as jnp
from jax import lax
from jax.experimental import pallas as pl
from jax.experimental.pallas import tpu as pltpu
from jax.sharding import PartitionSpec as P

TILE = 128
TPR = 5
HB = 8
CENTER = 6.5
RADIUS = 3.5
INFLATION_FACTOR = 0.8
GROUP = 8

F32 = jnp.float32
BF16 = jnp.bfloat16
VM = pltpu.VMEM
NT = (((1,), (1,)), ((), ()))
NN = (((1,), (0,)), ((), ()))
WHOLE = pl.BlockSpec(memory_space=VM)
SCALARS = pl.BlockSpec(memory_space=pltpu.SMEM)


def near(x):
    return pltpu.with_memory_space_constraint(x, VM)


def split(x):
    high = x.astype(BF16)
    return high, (x - high.astype(F32)).astype(BF16)


def stacked(x):
    return jnp.concatenate(split(x), axis=0)


def call(kernel, ins, outs, scratch=(), specs=None, flops=0, moved=0, name=None, out_vmem=True):
    out_shape = [VM(s, d) if out_vmem else jax.ShapeDtypeStruct(s, d) for s, d in outs]
    return pl.pallas_call(
        kernel,
        out_shape=out_shape,
        in_specs=specs,
        out_specs=[WHOLE] * len(outs),
        scratch_shapes=list(scratch),
        name=name,
        cost_estimate=pl.CostEstimate(flops=flops, bytes_accessed=moved, transcendentals=0),
        compiler_params=pltpu.CompilerParams(vmem_limit_bytes=6 << 20),
    )(*ins)


def prep_kernel(tiles_ref, out_ref, buffer_ref, semaphores):
    slots, step = buffer_ref.shape[:2]
    chunks = tiles_ref.shape[0] // step

    def copy(c):
        slot = lax.rem(c, slots)
        return pltpu.make_async_copy(
            tiles_ref.at[pl.ds(c * step, step)], buffer_ref.at[slot], semaphores.at[slot]
        )

    for c in range(slots):
        copy(c).start()

    def chunk(c, carry):
        copy(c).wait()
        slot = lax.rem(c, slots)
        for n in range(step):
            high, low = split(buffer_ref[slot, n].T)
            out_ref[c * step + n, :, :TILE] = high
            out_ref[c * step + n, :, TILE:] = low

        @pl.when(c + slots < chunks)
        def _():
            copy(c + slots).start()

        return carry

    lax.fori_loop(0, chunks, chunk, 0)


def prep(tiles):
    tiles = tiles.reshape(-1, TILE, TILE)
    slots, step = 5, 16
    return pl.pallas_call(
        prep_kernel,
        out_shape=VM((tiles.shape[0], TILE, 2 * TILE), BF16),
        in_specs=[pl.BlockSpec(memory_space=pltpu.HBM)],
        out_specs=WHOLE,
        scratch_shapes=[VM((slots, step, TILE, TILE), F32), pltpu.SemaphoreType.DMA((slots,))],
        name="prep",
        cost_estimate=pl.CostEstimate(flops=0, bytes_accessed=4 * tiles.size, transcendentals=0),
        compiler_params=pltpu.CompilerParams(vmem_limit_bytes=8 << 20),
    )(pltpu.with_memory_space_constraint(tiles, pltpu.HBM))


class Layout:
    def __init__(self, slices, blocks):
        most = slices * blocks * ((TPR - 1 + 1) // 2)
        room = most + GROUP + 2
        self.rows = slices * blocks * TPR
        self.tiles = self.rows + room
        self.places = self.tiles + 2 * room
        self.groups = self.places + 2 * room
        self.flags = self.groups + 1
        self.size = -(-(self.flags + 4) // 128) * 128


def plan_kernel(blocks_all, columns_ref, flags_ref, out_ref):
    slices, count = columns_ref.shape
    blocks = count // TPR
    at = Layout(slices, blocks)
    for i in range(4):
        out_ref[at.flags + i] = flags_ref[i]
    first_block = flags_ref[4]
    left_at = jnp.where(flags_ref[0] == 0, HB, 0)
    right_at = -left_at - blocks
    here = slices * blocks
    zero = slices * 2 * HB

    def row(i, units):
        s, r = i // blocks, i % blocks
        out_ref[at.rows + units] = i
        out_ref[at.rows + units + 1] = i
        found = jnp.int32(0)
        for n in range(TPR):
            where = columns_ref[s, r * TPR + n] - first_block + HB
            where = jnp.where(where < 0, where + blocks_all, where)
            where = jnp.where(where >= blocks_all, where - blocks_all, where)
            left = where < HB
            right = where >= HB + blocks
            away = jnp.logical_or(left, right)
            out_ref[i * TPR + n] = jnp.where(away, here, s * blocks + where - HB)
            if n > 0:
                out_ref[at.tiles + 2 * units + found] = i * TPR + n
                out_ref[at.places + 2 * units + found] = (
                    s * 2 * HB + where + jnp.where(right, right_at, left_at)
                )
                found = found + away.astype(jnp.int32)
        out_ref[at.tiles + 2 * units + found] = i * TPR
        out_ref[at.places + 2 * units + found] = zero
        return units + (found + 1) // 2

    units = lax.fori_loop(0, slices * blocks, row, jnp.int32(0), unroll=4)
    for n in range(GROUP):
        out_ref[at.rows + units + n] = 0
        for k in range(2):
            out_ref[at.tiles + 2 * (units + n) + k] = 0
            out_ref[at.places + 2 * (units + n) + k] = zero
    out_ref[at.groups] = (units + GROUP - 1) // GROUP


def plan(columns, flags, blocks_all):
    slices, count = columns.shape
    size = Layout(slices, count // TPR).size
    return pl.pallas_call(
        functools.partial(plan_kernel, blocks_all),
        out_shape=jax.ShapeDtypeStruct((size,), jnp.int32),
        in_specs=[SCALARS, SCALARS],
        out_specs=SCALARS,
        name="plan",
        compiler_params=pltpu.CompilerParams(vmem_limit_bytes=1 << 20),
    )(columns, flags)


def edges(flags, y_ref, inner_ref, outer_ref, near_ref, far_ref):
    width = HB * TILE
    points = y_ref.shape[2]
    final = y_ref.shape[0] - 1
    head = lambda: y_ref[:, :, :width]
    tail = lambda: y_ref[:, :, points - width :]
    first = lambda: y_ref[:1]
    last = lambda: y_ref[final:]
    for axis, inner, outer, low, high in (
        (0, inner_ref, outer_ref, head, tail),
        (1, near_ref, far_ref, first, last),
    ):

        @pl.when(flags[axis] == 0)
        def _(inner=inner, outer=outer, low=low, high=high):
            inner[...] = high()
            outer[...] = low()

        @pl.when(flags[axis] != 0)
        def _(inner=inner, outer=outer, low=low, high=high):
            inner[...] = low()
            outer[...] = high()


def edge_shapes(shape):
    slices, width, points = shape
    side = (slices, width, HB * TILE)
    return [(shape, F32), (side, F32), (side, F32), ((1, width, points), F32), ((1, width, points), F32)]


def start_kernel(odd_ref, x_ref, y_ref, *edge_refs):
    y_ref[...] = x_ref[...]
    edges([odd_ref[0], odd_ref[1]], y_ref, *edge_refs)


def start(odd, block):
    return call(
        start_kernel,
        [odd, block],
        edge_shapes(block.shape),
        specs=[SCALARS, WHOLE],
        moved=16 * block.size,
        name="start",
    )


def fold(product, width):
    return product[:width, :TILE] + product[:width, TILE:] + product[width:, :TILE]


def product(halves, tiles, width):
    left = jnp.concatenate(halves, axis=1)
    right = jnp.concatenate(tiles, axis=0)
    return fold(lax.dot_general(left, right, NN, preferred_element_type=F32), width)


def local_kernel(mode, scale, plan_ref, tiles_ref, y_ref, *refs):
    if mode in ("step", "gram"):
        previous_ref, out_ref, halves_ref = refs
    else:
        previous_ref, (out_ref, halves_ref) = None, refs
    slices, width, points = y_ref.shape
    blocks = points // TILE
    at = Layout(slices, blocks)
    for s in range(slices):
        for b in range(blocks):
            halves_ref[s * blocks + b] = stacked(y_ref[s, :, b * TILE : (b + 1) * TILE])
    halves_ref[slices * blocks] = jnp.zeros((2 * width, TILE), BF16)

    for s in range(slices):
        degree = 2.0
        if s == 0:
            degree = degree - jnp.where(plan_ref[at.flags + 2] != 0, 1.0, 0.0)
        if s == slices - 1:
            degree = degree - jnp.where(plan_ref[at.flags + 3] != 0, 1.0, 0.0)

        def row(r, carry, s=s, degree=degree):
            i = s * blocks + r
            halves = [halves_ref[plan_ref[i * TPR + n]] for n in range(TPR)]
            tiles = [tiles_ref[i * TPR + n] for n in range(TPR)]
            here = pl.ds(pl.multiple_of(r * TILE, TILE), TILE)
            y = y_ref[s, :, here]
            time = degree * y
            if s > 0:
                time = time - y_ref[s - 1, :, here]
            if s < slices - 1:
                time = time - y_ref[s + 1, :, here]
            image = product(halves, tiles, width) + INFLATION_FACTOR * time
            if mode != "image":
                image = (image - CENTER * y) * scale
            if previous_ref is not None:
                image = image - previous_ref[s, :, here]
            out_ref[s, :, here] = image
            return carry

        lax.fori_loop(0, blocks, row, 0, unroll=8)


def local_part(mode, scale, table, tiles, y, previous):
    slices, width, points = y.shape
    blocks = points // TILE
    ins = [table, near(tiles), near(y)] + ([] if previous is None else [near(previous)])
    return call(
        functools.partial(local_kernel, mode, scale),
        ins,
        [(y.shape, F32)],
        specs=[SCALARS] + [WHOLE] * (len(ins) - 1),
        scratch=[VM((slices * blocks + 1, 2 * width, TILE), BF16)],
        flops=2 * slices * blocks * TPR * 4 * width * TILE * TILE,
        moved=12 * y.size,
        name="local_" + mode,
    )[0]


def mix(matrix, y):
    high, low = split(matrix)
    y_high, y_low = split(y)
    left = jnp.concatenate([high, low, high], axis=1)
    right = jnp.concatenate([y_high, y_high, y_low], axis=0)
    return lax.dot_general(left, right, NN, preferred_element_type=F32)


def inner(left, right):
    width = left.shape[0]
    p = lax.dot_general(stacked(left), stacked(right), NT, preferred_element_type=F32)
    return (p[:width, :width] + p[width:, width:]) + (p[:width, width:] + p[width:, :width])


def folded(*matrices):
    width = matrices[0].shape[0]
    rows = width * width * len(matrices) // TILE
    flat = jnp.concatenate(matrices, axis=0)
    return jnp.concatenate([flat[i : i + rows] for i in range(0, flat.shape[0], rows)], axis=1)


def unfolded(block, width):
    flat = jnp.concatenate([block[:, i : i + width] for i in range(0, TILE, width)], axis=0)
    return [flat[i : i + width] for i in range(0, flat.shape[0], width)]


def finish_kernel(mode, scale, *refs):
    refs = list(refs)
    take = lambda n: [refs.pop(0) for _ in range(n)]
    plan_ref, tiles_ref, part_ref = take(3)
    inner_ref, outer_ref, near_ref, far_ref = take(4)
    if mode == "image":
        y_ref, matrix_ref, mixed_ref, gram_ref, halves_ref, new_ref = refs
    else:
        new_ref, *edge_refs = take(5)
        gram_ref = take(1)[0] if mode == "gram" else None
        (halves_ref,) = refs
    slices, width, points = part_ref.shape
    blocks = points // TILE
    at = Layout(slices, blocks)
    for s in range(slices):
        for b in range(HB):
            to = s * 2 * HB + b
            halves_ref[to] = stacked(inner_ref[s, :, b * TILE : (b + 1) * TILE])
            halves_ref[to + HB] = stacked(outer_ref[s, :, b * TILE : (b + 1) * TILE])
    halves_ref[slices * 2 * HB] = jnp.zeros((2 * width, TILE), BF16)

    time_odd = plan_ref[at.flags + 1] != 0
    factor = INFLATION_FACTOR * scale
    for s in range(slices):
        image = part_ref[s]
        if s == 0:
            before = jnp.where(time_odd, near_ref[0], far_ref[0])
            image = image - jnp.where(plan_ref[at.flags + 2] != 0, 0.0, factor * before)
        if s == slices - 1:
            after = jnp.where(time_odd, far_ref[0], near_ref[0])
            image = image - jnp.where(plan_ref[at.flags + 3] != 0, 0.0, factor * after)
        new_ref[s] = image

    def group(g, carry):
        done = []
        for k in range(GROUP):
            u = g * GROUP + k
            halves = [halves_ref[plan_ref[at.places + 2 * u + j]] for j in range(2)]
            tiles = [plan_ref[at.tiles + 2 * u + j] for j in range(2)]
            tiles = [tiles_ref[t] for t in tiles]
            done.append((plan_ref[at.rows + u], product(halves, tiles, width)))
        for i, value in done:
            here = pl.ds(pl.multiple_of((i % blocks) * TILE, TILE), TILE)
            new_ref[i // blocks, :, here] += scale * value
        return carry

    lax.fori_loop(0, plan_ref[at.groups], group, 0)

    if mode != "image":
        edges([plan_ref[at.flags], plan_ref[at.flags + 1]], new_ref, *edge_refs)
    if mode == "gram":
        gram_ref[...] = folded(sum(inner(new_ref[s], new_ref[s]) for s in range(slices)))
    if mode == "image":
        matrix = matrix_ref[...]
        first, second = 0.0, 0.0
        for s in range(slices):
            mixed = mix(matrix, y_ref[s])
            mixed_ref[s] = mixed
            first = first + inner(mixed, mixed)
            second = second + inner(mixed, mix(matrix, new_ref[s]))
        gram_ref[...] = folded(first, second)


def finish(mode, scale, table, tiles, part, y, halo, matrix=None):
    slices, width, points = y.shape
    blocks = points // TILE
    ins = [table] + [near(v) for v in (tiles, part, *halo)]
    if mode == "image":
        ins += [near(y), near(matrix)]
        outs = [(y.shape, F32), ((2 * width * width // TILE, TILE), F32)]
    else:
        outs = edge_shapes(y.shape)
    if mode == "gram":
        outs = outs + [((width * width // TILE, TILE), F32)]
    scratch = [VM((slices * 2 * HB + 1, 2 * width, TILE), BF16)]
    if mode == "image":
        scratch.append(VM(y.shape, F32))
    return call(
        functools.partial(finish_kernel, mode, scale),
        ins,
        outs,
        scratch=scratch,
        specs=[SCALARS] + [WHOLE] * (len(ins) - 1),
        flops=2 * slices * blocks * 2 * 4 * width * TILE * TILE,
        moved=24 * y.size,
        name="finish_" + mode,
    )


def inverse_factor(gram):
    width = gram.shape[0]
    rows = lax.broadcasted_iota(jnp.int32, (width, width), 0)
    columns = lax.broadcasted_iota(jnp.int32, (width, width), 1)
    inverse = (rows == columns).astype(F32)
    row_of = lax.broadcasted_iota(jnp.int32, (width, 1), 0)
    for j in range(width):
        root = lax.rsqrt(gram[j : j + 1, j : j + 1])
        gram_row = gram[j : j + 1, :] * root
        inverse_row = inverse[j : j + 1, :] * root
        column = jnp.where(row_of > j, gram[:, j : j + 1] * root, 0.0)
        gram = gram - column * gram_row
        inverse = jnp.where(row_of == j, inverse_row, inverse - column * inverse_row)
    return inverse


def factor_kernel(count, gram_ref, out_ref):
    (gram,) = unfolded(gram_ref[...] * (1.0 / count), out_ref.shape[0])
    out_ref[...] = inverse_factor(gram)


def factor(gram, width, count):
    return call(
        functools.partial(factor_kernel, float(count)),
        [near(gram)],
        [((width, width), F32)],
        specs=[WHOLE],
        flops=40000 * gram.size,
        moved=8 * gram.size,
        name="factor",
    )[0]


def basis_kernel(matrix_ref, y_ref, out_ref):
    for s in range(y_ref.shape[0]):
        out_ref[s] = mix(matrix_ref[...], y_ref[s])


def basis(matrix, y):
    return call(
        basis_kernel,
        [near(matrix), near(y)],
        [(y.shape, F32)],
        specs=[WHOLE] * 2,
        flops=2 * matrix.shape[0] * y.size,
        moved=8 * y.size,
        name="basis",
        out_vmem=False,
    )[0]


def close_kernel(count, sums_ref, y_ref, basis_ref, ritz_ref):
    high = lax.Precision.HIGHEST
    gram, projected = unfolded(sums_ref[...] * (1.0 / count), ritz_ref.shape[0])
    matrix = inverse_factor(gram)
    for s in range(y_ref.shape[0]):
        basis_ref[s] = mix(matrix, y_ref[s])
    half = lax.dot_general(matrix, projected, NN, precision=high, preferred_element_type=F32)
    ritz_ref[...] = lax.dot_general(half, matrix, NT, precision=high, preferred_element_type=F32)


def close(sums, y, count):
    width = y.shape[1]
    return call(
        functools.partial(close_kernel, float(count)),
        [near(sums), near(y)],
        [(y.shape, F32), ((width, width), F32)],
        specs=[WHOLE] * 2,
        flops=2 * width * y.size,
        moved=8 * y.size,
        name="close",
        out_vmem=False,
    )


def stages_of(axis):
    count = lax.axis_size(axis)
    found, stride = [], 1
    if (count.bit_length() - 1) % 2:
        found, stride = [(axis, (1,))], 2
    while stride < count:
        found.append((axis, (stride, 2 * stride, 3 * stride)))
        stride *= 4
    return found


def pairs_of(axis):
    return [(axis, (1 << k,)) for k in range((lax.axis_size(axis) - 1).bit_length())]


def add_over(value, stages):
    for axis, strides in stages:
        count = lax.axis_size(axis)
        others = [lax.ppermute(value, axis, [(i, i ^ k) for i in range(count)]) for k in strides]
        if len(others) == 1:
            value = value + others[0]
        else:
            value = (value + others[0]) + (others[1] + others[2])
    return value


def inner_pairs(axis):
    count = lax.axis_size(axis)
    return [(i, i ^ 1) for i in range(count)]


def outer_pairs(axis):
    count = lax.axis_size(axis)
    return [(i, (i + 1) % count if i % 2 else (i - 1) % count) for i in range(count)]


def exchange(edge):
    inner, outer, near_slice, far_slice = edge
    inner = lax.ppermute(inner, "space", inner_pairs("space"))
    outer = lax.ppermute(outer, "space", outer_pairs("space"))
    far_slice = lax.ppermute(far_slice, "tm", outer_pairs("tm"))
    near_slice = lax.ppermute(near_slice, "tm", inner_pairs("tm"))
    return inner, outer, near_slice, far_slice


def body(start_block, stiffness_tiles, tile_columns):
    slices, width, local_points = start_block.shape
    local_blocks = local_points // TILE
    blocks_all = lax.axis_size("space") * local_blocks
    count_all = slices * local_points * lax.axis_size("tm") * lax.axis_size("space")
    time_index = lax.axis_index("tm")
    ends = (time_index == 0, time_index == lax.axis_size("tm") - 1)
    space_index = lax.axis_index("space")
    odd = jnp.stack(
        [
            space_index % 2,
            time_index % 2,
            ends[0].astype(jnp.int32),
            ends[1].astype(jnp.int32),
            space_index * local_blocks,
        ]
    )

    y, *edge = start(odd, start_block)
    table = plan(tile_columns, odd, blocks_all)
    tiles = prep(stiffness_tiles)

    across, along = pairs_of("space"), pairs_of("tm")
    half = -(-len(across) // 2)
    early = [along[:1] + across[:half], across[half:], along[1:-1], along[-1:]]

    def apply(mode, scale, y, edge, previous=None, beside=None):
        halo = exchange(edge)
        part = local_part(mode, scale, table, tiles, y, previous)
        extra = None
        if beside is not None:
            part, extra = lax.optimization_barrier((part, beside[0]))
            part, extra = lax.optimization_barrier((part, beside[1](extra)))
        return finish(mode, scale, table, tiles, part, y, halo, extra), extra

    (y1, *edge), _ = apply("first", 1.0 / RADIUS, y, edge)
    (y2, *edge), _ = apply("step", 2.0 / RADIUS, y1, edge, y)
    (filtered, *edge, gram), _ = apply("gram", 2.0 / RADIUS, y2, edge, y1)

    def stage(n):
        return lambda gram: add_over(gram, early[n])

    (y1, *edge), gram = apply("first", 1.0 / RADIUS, filtered, edge, None, (gram, stage(0)))
    (y2, *edge), gram = apply("step", 2.0 / RADIUS, y1, edge, filtered, (gram, stage(1)))
    (y3, *edge), gram = apply("step", 2.0 / RADIUS, y2, edge, y1, (gram, stage(2)))
    (second, sums), matrix = apply(
        "image", 1.0, y3, edge, None, (gram, lambda gram: factor(stage(3)(gram), width, count_all))
    )
    first_basis = basis(matrix, filtered)
    sums = add_over(sums, stages_of("tm") + stages_of("space"))
    ritz_basis, ritz_matrix = close(sums, second, count_all)
    return ritz_basis, first_basis, ritz_matrix


def solution(mesh):
    placed = (P("tm", None, "space"), P("tm", "space", None, None), P("tm", "space"))
    return jax.shard_map(
        body,
        mesh=mesh,
        in_specs=placed,
        out_specs=(P("tm", None, "space"), P("tm", None, "space"), P()),
        check_vma=False,
    )
```

```python
import functools

import jax
import jax.numpy as jnp
from jax import lax
from jax.experimental import pallas as pl
from jax.experimental.pallas import tpu as pltpu
from jax.sharding import PartitionSpec as P

TILE = 128
TPR = 5
HB = 8
CENTER = 6.5
RADIUS = 3.5
INFLATION_FACTOR = 0.8
GROUP = 12

F32 = jnp.float32
BF16 = jnp.bfloat16
VM = pltpu.VMEM
NT = (((1,), (1,)), ((), ()))
NN = (((1,), (0,)), ((), ()))
WHOLE = pl.BlockSpec(memory_space=VM)
SCALARS = pl.BlockSpec(memory_space=pltpu.SMEM)


def near(x):
    return pltpu.with_memory_space_constraint(x, VM)


def split(x):
    high = x.astype(BF16)
    return high, (x - high.astype(F32)).astype(BF16)


def stacked(x):
    return jnp.concatenate(split(x), axis=0)


def call(kernel, ins, outs, scratch=(), specs=None, flops=0, moved=0, name=None, out_vmem=True):
    out_shape = [VM(s, d) if out_vmem else jax.ShapeDtypeStruct(s, d) for s, d in outs]
    return pl.pallas_call(
        kernel,
        out_shape=out_shape,
        in_specs=specs,
        out_specs=[WHOLE] * len(outs),
        scratch_shapes=list(scratch),
        name=name,
        cost_estimate=pl.CostEstimate(flops=flops, bytes_accessed=moved, transcendentals=0),
        compiler_params=pltpu.CompilerParams(vmem_limit_bytes=6 << 20),
    )(*ins)


def prep_kernel(tiles_ref, out_ref, buffer_ref, semaphores):
    slots, step = buffer_ref.shape[:2]
    chunks = tiles_ref.shape[0] // step

    def copy(c):
        slot = lax.rem(c, slots)
        return pltpu.make_async_copy(
            tiles_ref.at[pl.ds(c * step, step)], buffer_ref.at[slot], semaphores.at[slot]
        )

    for c in range(slots):
        copy(c).start()

    def chunk(c, carry):
        copy(c).wait()
        slot = lax.rem(c, slots)
        for n in range(step):
            high, low = split(buffer_ref[slot, n].T)
            out_ref[c * step + n, :, :TILE] = high
            out_ref[c * step + n, :, TILE:] = low

        @pl.when(c + slots < chunks)
        def _():
            copy(c + slots).start()

        return carry

    lax.fori_loop(0, chunks, chunk, 0)


def prep(tiles):
    tiles = tiles.reshape(-1, TILE, TILE)
    slots, step = 5, 16
    return pl.pallas_call(
        prep_kernel,
        out_shape=VM((tiles.shape[0], TILE, 2 * TILE), BF16),
        in_specs=[pl.BlockSpec(memory_space=pltpu.HBM)],
        out_specs=WHOLE,
        scratch_shapes=[VM((slots, step, TILE, TILE), F32), pltpu.SemaphoreType.DMA((slots,))],
        name="prep",
        cost_estimate=pl.CostEstimate(flops=0, bytes_accessed=4 * tiles.size, transcendentals=0),
        compiler_params=pltpu.CompilerParams(vmem_limit_bytes=8 << 20),
    )(pltpu.with_memory_space_constraint(tiles, pltpu.HBM))


class Layout:
    def __init__(self, slices, blocks):
        most = slices * blocks * ((TPR - 1 + 1) // 2)
        room = most + GROUP + 2
        self.rows = slices * blocks * TPR
        self.tiles = self.rows + room
        self.places = self.tiles + 2 * room
        self.groups = self.places + 2 * room
        self.flags = self.groups + 1
        self.size = -(-(self.flags + 4) // 128) * 128


def plan_kernel(blocks_all, columns_ref, flags_ref, out_ref):
    slices, count = columns_ref.shape
    blocks = count // TPR
    at = Layout(slices, blocks)
    for i in range(4):
        out_ref[at.flags + i] = flags_ref[i]
    first_block = flags_ref[4]
    left_at = jnp.where(flags_ref[0] == 0, HB, 0)
    right_at = -left_at - blocks
    here = slices * blocks
    zero = slices * 2 * HB

    def row(i, units):
        s, r = i // blocks, i % blocks
        out_ref[at.rows + units] = i
        out_ref[at.rows + units + 1] = i
        found = jnp.int32(0)
        for n in range(TPR):
            where = columns_ref[s, r * TPR + n] - first_block + HB
            where = jnp.where(where < 0, where + blocks_all, where)
            where = jnp.where(where >= blocks_all, where - blocks_all, where)
            left = where < HB
            right = where >= HB + blocks
            away = jnp.logical_or(left, right)
            out_ref[i * TPR + n] = jnp.where(away, here, s * blocks + where - HB)
            if n > 0:
                out_ref[at.tiles + 2 * units + found] = i * TPR + n
                out_ref[at.places + 2 * units + found] = (
                    s * 2 * HB + where + jnp.where(right, right_at, left_at)
                )
                found = found + away.astype(jnp.int32)
        out_ref[at.tiles + 2 * units + found] = i * TPR
        out_ref[at.places + 2 * units + found] = zero
        return units + (found + 1) // 2

    units = lax.fori_loop(0, slices * blocks, row, jnp.int32(0), unroll=4)
    for n in range(GROUP):
        out_ref[at.rows + units + n] = 0
        for k in range(2):
            out_ref[at.tiles + 2 * (units + n) + k] = 0
            out_ref[at.places + 2 * (units + n) + k] = zero
    out_ref[at.groups] = (units + GROUP - 1) // GROUP


def plan(columns, flags, blocks_all):
    slices, count = columns.shape
    size = Layout(slices, count // TPR).size
    return pl.pallas_call(
        functools.partial(plan_kernel, blocks_all),
        out_shape=pltpu.SMEM((size,), jnp.int32),
        in_specs=[SCALARS, SCALARS],
        out_specs=SCALARS,
        name="plan",
        compiler_params=pltpu.CompilerParams(vmem_limit_bytes=1 << 20),
    )(columns, flags)


def edges(flags, y_ref, inner_ref, outer_ref, near_ref, far_ref):
    width = HB * TILE
    points = y_ref.shape[2]
    final = y_ref.shape[0] - 1
    head = lambda: y_ref[:, :, :width]
    tail = lambda: y_ref[:, :, points - width :]
    first = lambda: y_ref[:1]
    last = lambda: y_ref[final:]
    for axis, inner, outer, low, high in (
        (0, inner_ref, outer_ref, head, tail),
        (1, near_ref, far_ref, first, last),
    ):

        @pl.when(flags[axis] == 0)
        def _(inner=inner, outer=outer, low=low, high=high):
            inner[...] = high()
            outer[...] = low()

        @pl.when(flags[axis] != 0)
        def _(inner=inner, outer=outer, low=low, high=high):
            inner[...] = low()
            outer[...] = high()


def edge_shapes(shape):
    slices, width, points = shape
    side = (slices, width, HB * TILE)
    return [(shape, F32), (side, F32), (side, F32), ((1, width, points), F32), ((1, width, points), F32)]


def start_kernel(odd_ref, x_ref, y_ref, *edge_refs):
    y_ref[...] = x_ref[...]
    edges([odd_ref[0], odd_ref[1]], y_ref, *edge_refs)


def start(odd, block):
    return call(
        start_kernel,
        [odd, block],
        edge_shapes(block.shape),
        specs=[SCALARS, WHOLE],
        moved=16 * block.size,
        name="start",
    )


def fold(product, width):
    return product[:width, :TILE] + product[:width, TILE:] + product[width:, :TILE]


def product(halves, tiles, width):
    left = jnp.concatenate(halves, axis=1)
    right = jnp.concatenate(tiles, axis=0)
    return fold(lax.dot_general(left, right, NN, preferred_element_type=F32), width)


def local_kernel(mode, scale, plan_ref, tiles_ref, y_ref, *refs):
    if mode in ("step", "gram"):
        previous_ref, out_ref, halves_ref = refs
    else:
        previous_ref, (out_ref, halves_ref) = None, refs
    slices, width, points = y_ref.shape
    blocks = points // TILE
    at = Layout(slices, blocks)
    for s in range(slices):
        for b in range(blocks):
            halves_ref[s * blocks + b] = stacked(y_ref[s, :, b * TILE : (b + 1) * TILE])
    halves_ref[slices * blocks] = jnp.zeros((2 * width, TILE), BF16)

    for s in range(slices):
        degree = 2.0
        if s == 0:
            degree = degree - jnp.where(plan_ref[at.flags + 2] != 0, 1.0, 0.0)
        if s == slices - 1:
            degree = degree - jnp.where(plan_ref[at.flags + 3] != 0, 1.0, 0.0)

        def row(r, carry, s=s, degree=degree):
            i = s * blocks + r
            halves = [halves_ref[plan_ref[i * TPR + n]] for n in range(TPR)]
            tiles = [tiles_ref[i * TPR + n] for n in range(TPR)]
            here = pl.ds(pl.multiple_of(r * TILE, TILE), TILE)
            y = y_ref[s, :, here]
            time = degree * y
            if s > 0:
                time = time - y_ref[s - 1, :, here]
            if s < slices - 1:
                time = time - y_ref[s + 1, :, here]
            image = product(halves, tiles, width) + INFLATION_FACTOR * time
            if mode != "image":
                image = (image - CENTER * y) * scale
            if previous_ref is not None:
                image = image - previous_ref[s, :, here]
            out_ref[s, :, here] = image
            return carry

        lax.fori_loop(0, blocks, row, 0, unroll=16)


def local_part(mode, scale, table, tiles, y, previous):
    slices, width, points = y.shape
    blocks = points // TILE
    ins = [table, near(tiles), near(y)] + ([] if previous is None else [near(previous)])
    return call(
        functools.partial(local_kernel, mode, scale),
        ins,
        [(y.shape, F32)],
        specs=[SCALARS] + [WHOLE] * (len(ins) - 1),
        scratch=[VM((slices * blocks + 1, 2 * width, TILE), BF16)],
        flops=2 * slices * blocks * TPR * 4 * width * TILE * TILE,
        moved=12 * y.size,
        name="local_" + mode,
    )[0]


def mix(matrix, y):
    high, low = split(matrix)
    y_high, y_low = split(y)
    left = jnp.concatenate([high, low, high], axis=1)
    right = jnp.concatenate([y_high, y_high, y_low], axis=0)
    return lax.dot_general(left, right, NN, preferred_element_type=F32)


def inner(left, right):
    width = left.shape[0]
    p = lax.dot_general(stacked(left), stacked(right), NT, preferred_element_type=F32)
    return (p[:width, :width] + p[width:, width:]) + (p[:width, width:] + p[width:, :width])


def folded(*matrices):
    width = matrices[0].shape[0]
    rows = width * width * len(matrices) // TILE
    flat = jnp.concatenate(matrices, axis=0)
    return jnp.concatenate([flat[i : i + rows] for i in range(0, flat.shape[0], rows)], axis=1)


def unfolded(block, width):
    flat = jnp.concatenate([block[:, i : i + width] for i in range(0, TILE, width)], axis=0)
    return [flat[i : i + width] for i in range(0, flat.shape[0], width)]


def finish_kernel(mode, scale, *refs):
    refs = list(refs)
    take = lambda n: [refs.pop(0) for _ in range(n)]
    plan_ref, tiles_ref, part_ref = take(3)
    inner_ref, outer_ref, near_ref, far_ref = take(4)
    if mode == "image":
        y_ref, matrix_ref, mixed_ref, gram_ref, halves_ref, new_ref = refs
    else:
        new_ref, *edge_refs = take(5)
        gram_ref = take(1)[0] if mode == "gram" else None
        (halves_ref,) = refs
    slices, width, points = part_ref.shape
    blocks = points // TILE
    at = Layout(slices, blocks)
    for s in range(slices):
        for b in range(HB):
            to = s * 2 * HB + b
            halves_ref[to] = stacked(inner_ref[s, :, b * TILE : (b + 1) * TILE])
            halves_ref[to + HB] = stacked(outer_ref[s, :, b * TILE : (b + 1) * TILE])
    halves_ref[slices * 2 * HB] = jnp.zeros((2 * width, TILE), BF16)

    time_odd = plan_ref[at.flags + 1] != 0
    factor = INFLATION_FACTOR * scale
    for s in range(slices):
        image = part_ref[s]
        if s == 0:
            before = jnp.where(time_odd, near_ref[0], far_ref[0])
            image = image - jnp.where(plan_ref[at.flags + 2] != 0, 0.0, factor * before)
        if s == slices - 1:
            after = jnp.where(time_odd, far_ref[0], near_ref[0])
            image = image - jnp.where(plan_ref[at.flags + 3] != 0, 0.0, factor * after)
        new_ref[s] = image

    def group(g, carry):
        done = []
        for k in range(GROUP):
            u = g * GROUP + k
            halves = [halves_ref[plan_ref[at.places + 2 * u + j]] for j in range(2)]
            tiles = [plan_ref[at.tiles + 2 * u + j] for j in range(2)]
            tiles = [tiles_ref[t] for t in tiles]
            done.append((plan_ref[at.rows + u], product(halves, tiles, width)))
        for i, value in done:
            here = pl.ds(pl.multiple_of((i % blocks) * TILE, TILE), TILE)
            new_ref[i // blocks, :, here] += scale * value
        return carry

    lax.fori_loop(0, plan_ref[at.groups], group, 0)

    if mode != "image":
        edges([plan_ref[at.flags], plan_ref[at.flags + 1]], new_ref, *edge_refs)
    if mode == "gram":
        gram_ref[...] = folded(sum(inner(new_ref[s], new_ref[s]) for s in range(slices)))
    if mode == "image":
        matrix = matrix_ref[...]
        first, second = 0.0, 0.0
        for s in range(slices):
            mixed = mix(matrix, y_ref[s])
            mixed_ref[s] = mixed
            first = first + inner(mixed, mixed)
            second = second + inner(mixed, mix(matrix, new_ref[s]))
        gram_ref[...] = folded(first, second)


def finish(mode, scale, table, tiles, part, y, halo, matrix=None):
    slices, width, points = y.shape
    blocks = points // TILE
    ins = [table] + [near(v) for v in (tiles, part, *halo)]
    if mode == "image":
        ins += [near(y), near(matrix)]
        outs = [(y.shape, F32), ((2 * width * width // TILE, TILE), F32)]
    else:
        outs = edge_shapes(y.shape)
    if mode == "gram":
        outs = outs + [((width * width // TILE, TILE), F32)]
    scratch = [VM((slices * 2 * HB + 1, 2 * width, TILE), BF16)]
    if mode == "image":
        scratch.append(VM(y.shape, F32))
    return call(
        functools.partial(finish_kernel, mode, scale),
        ins,
        outs,
        scratch=scratch,
        specs=[SCALARS] + [WHOLE] * (len(ins) - 1),
        flops=2 * slices * blocks * 2 * 4 * width * TILE * TILE,
        moved=24 * y.size,
        name="finish_" + mode,
    )


def inverse_factor(gram):
    width = gram.shape[0]
    square = (width, width)
    rows = lax.broadcasted_iota(jnp.int32, square, 0)
    columns = lax.broadcasted_iota(jnp.int32, square, 1)
    inverse = (rows == columns).astype(F32)
    column = jnp.broadcast_to(gram[:, :1], square)
    for j in range(width - 1):
        following = jnp.broadcast_to(gram[:, j + 1 : j + 2], square)
        scaled = jnp.where(rows > j, column, 0.0) * (1.0 / column[j : j + 1])
        gram = gram - scaled * gram[j : j + 1]
        inverse = inverse - scaled * inverse[j : j + 1]
        column = following - scaled * column[j + 1 : j + 2]
    pivots = jnp.sum(jnp.where(rows == columns, gram, 0.0), axis=1, keepdims=True)
    return inverse * lax.rsqrt(pivots)


def factor_kernel(count, gram_ref, out_ref):
    (gram,) = unfolded(gram_ref[...] * (1.0 / count), out_ref.shape[0])
    out_ref[...] = inverse_factor(gram)


def factor(gram, width, count):
    return call(
        functools.partial(factor_kernel, float(count)),
        [near(gram)],
        [((width, width), F32)],
        specs=[WHOLE],
        flops=40000 * gram.size,
        moved=8 * gram.size,
        name="factor",
    )[0]


def basis_kernel(matrix_ref, y_ref, out_ref):
    for s in range(y_ref.shape[0]):
        out_ref[s] = mix(matrix_ref[...], y_ref[s])


def basis(matrix, y):
    return call(
        basis_kernel,
        [near(matrix), near(y)],
        [(y.shape, F32)],
        specs=[WHOLE] * 2,
        flops=2 * matrix.shape[0] * y.size,
        moved=8 * y.size,
        name="basis",
        out_vmem=False,
    )[0]


def close_kernel(count, sums_ref, y_ref, basis_ref, ritz_ref):
    high = lax.Precision.HIGHEST
    gram, projected = unfolded(sums_ref[...] * (1.0 / count), ritz_ref.shape[0])
    matrix = inverse_factor(gram)
    for s in range(y_ref.shape[0]):
        basis_ref[s] = mix(matrix, y_ref[s])
    half = lax.dot_general(matrix, projected, NN, precision=high, preferred_element_type=F32)
    ritz_ref[...] = lax.dot_general(half, matrix, NT, precision=high, preferred_element_type=F32)


def close(sums, y, count):
    width = y.shape[1]
    return call(
        functools.partial(close_kernel, float(count)),
        [near(sums), near(y)],
        [(y.shape, F32), ((width, width), F32)],
        specs=[WHOLE] * 2,
        flops=2 * width * y.size,
        moved=8 * y.size,
        name="close",
        out_vmem=False,
    )


def stages_of(axis):
    count = lax.axis_size(axis)
    found, stride = [], 1
    if (count.bit_length() - 1) % 2:
        found, stride = [(axis, (1,))], 2
    while stride < count:
        found.append((axis, (stride, 2 * stride, 3 * stride)))
        stride *= 4
    return found


def pairs_of(axis):
    return [(axis, (1 << k,)) for k in range((lax.axis_size(axis) - 1).bit_length())]


def add_over(value, stages):
    for axis, strides in stages:
        count = lax.axis_size(axis)
        others = [lax.ppermute(value, axis, [(i, i ^ k) for i in range(count)]) for k in strides]
        if len(others) == 1:
            value = value + others[0]
        else:
            value = (value + others[0]) + (others[1] + others[2])
    return value


def inner_pairs(axis):
    count = lax.axis_size(axis)
    return [(i, i ^ 1) for i in range(count)]


def outer_pairs(axis):
    count = lax.axis_size(axis)
    return [(i, (i + 1) % count if i % 2 else (i - 1) % count) for i in range(count)]


def exchange(edge):
    inner, outer, near_slice, far_slice = edge
    inner = lax.ppermute(inner, "space", inner_pairs("space"))
    outer = lax.ppermute(outer, "space", outer_pairs("space"))
    far_slice = lax.ppermute(far_slice, "tm", outer_pairs("tm"))
    near_slice = lax.ppermute(near_slice, "tm", inner_pairs("tm"))
    return inner, outer, near_slice, far_slice


def body(start_block, stiffness_tiles, tile_columns):
    slices, width, local_points = start_block.shape
    local_blocks = local_points // TILE
    blocks_all = lax.axis_size("space") * local_blocks
    count_all = slices * local_points * lax.axis_size("tm") * lax.axis_size("space")
    time_index = lax.axis_index("tm")
    ends = (time_index == 0, time_index == lax.axis_size("tm") - 1)
    space_index = lax.axis_index("space")
    odd = jnp.stack(
        [
            space_index % 2,
            time_index % 2,
            ends[0].astype(jnp.int32),
            ends[1].astype(jnp.int32),
            space_index * local_blocks,
        ]
    )

    y, *edge = start(odd, start_block)
    table = plan(tile_columns, odd, blocks_all)
    tiles = prep(stiffness_tiles)

    across, along = pairs_of("space"), pairs_of("tm")
    half = -(-len(across) // 2)
    early = [along[:1] + across[:half], across[half:], along[1:-1], along[-1:]]

    def apply(mode, scale, y, edge, previous=None, beside=None):
        halo = exchange(edge)
        part = local_part(mode, scale, table, tiles, y, previous)
        extra = None
        if beside is not None:
            part, extra = lax.optimization_barrier((part, beside[0]))
            part, extra = lax.optimization_barrier((part, beside[1](extra)))
        return finish(mode, scale, table, tiles, part, y, halo, extra), extra

    (y1, *edge), _ = apply("first", 1.0 / RADIUS, y, edge)
    (y2, *edge), _ = apply("step", 2.0 / RADIUS, y1, edge, y)
    (filtered, *edge, gram), _ = apply("gram", 2.0 / RADIUS, y2, edge, y1)

    def stage(n):
        return lambda gram: add_over(gram, early[n])

    (y1, *edge), gram = apply("first", 1.0 / RADIUS, filtered, edge, None, (gram, stage(0)))
    (y2, *edge), gram = apply("step", 2.0 / RADIUS, y1, edge, filtered, (gram, stage(1)))
    (y3, *edge), gram = apply("step", 2.0 / RADIUS, y2, edge, y1, (gram, stage(2)))
    (second, sums), matrix = apply(
        "image", 1.0, y3, edge, None, (gram, lambda gram: factor(stage(3)(gram), width, count_all))
    )
    first_basis = basis(matrix, filtered)
    sums = add_over(sums, stages_of("tm") + stages_of("space"))
    ritz_basis, ritz_matrix = close(sums, second, count_all)
    return ritz_basis, first_basis, ritz_matrix


def solution(mesh):
    placed = (P("tm", None, "space"), P("tm", "space", None, None), P("tm", "space"))
    return jax.shard_map(
        body,
        mesh=mesh,
        in_specs=placed,
        out_specs=(P("tm", None, "space"), P("tm", None, "space"), P()),
        check_vma=False,
    )
```

```python
import functools

import jax
import jax.numpy as jnp
from jax import lax
from jax.experimental import pallas as pl
from jax.experimental.pallas import tpu as pltpu
from jax.sharding import PartitionSpec as P

TILE = 128
TPR = 5
HB = 8
CENTER = 6.5
RADIUS = 3.5
INFLATION_FACTOR = 0.8
GROUP = 8

F32 = jnp.float32
BF16 = jnp.bfloat16
VM = pltpu.VMEM
NT = (((1,), (1,)), ((), ()))
NN = (((1,), (0,)), ((), ()))
WHOLE = pl.BlockSpec(memory_space=VM)
SCALARS = pl.BlockSpec(memory_space=pltpu.SMEM)


def near(x):
    return pltpu.with_memory_space_constraint(x, VM)


def split(x):
    high = x.astype(BF16)
    return high, (x - high.astype(F32)).astype(BF16)


def stacked(x):
    return jnp.concatenate(split(x), axis=0)


def call(kernel, ins, outs, scratch=(), specs=None, flops=0, moved=0, name=None, out_vmem=True, aliases=None):
    out_shape = [VM(s, d) if out_vmem else jax.ShapeDtypeStruct(s, d) for s, d in outs]
    return pl.pallas_call(
        kernel,
        out_shape=out_shape,
        in_specs=specs,
        out_specs=[WHOLE] * len(outs),
        scratch_shapes=list(scratch),
        name=name,
        input_output_aliases=aliases or {},
        cost_estimate=pl.CostEstimate(flops=flops, bytes_accessed=moved, transcendentals=0),
        compiler_params=pltpu.CompilerParams(vmem_limit_bytes=6 << 20),
    )(*ins)


def prep_kernel(tiles_ref, out_ref, buffer_ref, semaphores):
    slots, step = buffer_ref.shape[:2]
    chunks = tiles_ref.shape[0] // step

    def copy(c):
        slot = lax.rem(c, slots)
        return pltpu.make_async_copy(
            tiles_ref.at[pl.ds(c * step, step)], buffer_ref.at[slot], semaphores.at[slot]
        )

    for c in range(slots):
        copy(c).start()

    def chunk(c, carry):
        copy(c).wait()
        slot = lax.rem(c, slots)
        for n in range(step):
            high, low = split(buffer_ref[slot, n].T)
            out_ref[c * step + n, :, :TILE] = high
            out_ref[c * step + n, :, TILE:] = low

        @pl.when(c + slots < chunks)
        def _():
            copy(c + slots).start()

        return carry

    lax.fori_loop(0, chunks, chunk, 0)


def prep(tiles):
    tiles = tiles.reshape(-1, TILE, TILE)
    slots, step = 5, 16
    return pl.pallas_call(
        prep_kernel,
        out_shape=VM((tiles.shape[0], TILE, 2 * TILE), BF16),
        in_specs=[pl.BlockSpec(memory_space=pltpu.HBM)],
        out_specs=WHOLE,
        scratch_shapes=[VM((slots, step, TILE, TILE), F32), pltpu.SemaphoreType.DMA((slots,))],
        name="prep",
        cost_estimate=pl.CostEstimate(flops=0, bytes_accessed=4 * tiles.size, transcendentals=0),
        compiler_params=pltpu.CompilerParams(vmem_limit_bytes=8 << 20),
    )(pltpu.with_memory_space_constraint(tiles, pltpu.HBM))


class Layout:
    def __init__(self, slices, blocks):
        self.half = blocks // 2
        self.room = slices * self.half * (TPR // 2) + GROUP + 2
        self.rows = slices * blocks * TPR
        self.tiles = self.rows + 2 * self.room
        self.places = self.tiles + 4 * self.room
        self.groups = self.places + 4 * self.room
        self.flags = self.groups + 2
        self.size = -(-(self.flags + 4) // 128) * 128


def plan_kernel(blocks_all, columns_ref, flags_ref, out_ref):
    slices, count = columns_ref.shape
    blocks = count // TPR
    at = Layout(slices, blocks)
    for i in range(4):
        out_ref[at.flags + i] = flags_ref[i]
    first_block = flags_ref[4]
    here = slices * blocks
    zero = slices * HB
    for side in range(2):
        rows = at.rows + side * at.room
        tiles = at.tiles + side * 2 * at.room
        places = at.places + side * 2 * at.room
        units = jnp.int32(0)
        for s in range(slices):

            def row(k, units, s=s, side=side, rows=rows, tiles=tiles, places=places):
                r = side * at.half + k
                i = s * blocks + r
                out_ref[rows + units] = s * at.half + k
                out_ref[rows + units + 1] = s * at.half + k
                found = jnp.int32(0)
                for n in range(TPR):
                    where = columns_ref[s, r * TPR + n] - first_block + HB
                    where = jnp.where(where < 0, where + blocks_all, where)
                    where = jnp.where(where >= blocks_all, where - blocks_all, where)
                    away = where >= HB + blocks if side else where < HB
                    out_ref[i * TPR + n] = jnp.where(away, here, s * blocks + where - HB)
                    if n > 0:
                        out_ref[tiles + 2 * units + found] = i * TPR + n
                        out_ref[places + 2 * units + found] = s * HB + where - side * (HB + blocks)
                        found = found + away.astype(jnp.int32)
                out_ref[tiles + 2 * units + found] = i * TPR
                out_ref[places + 2 * units + found] = zero
                return units + (found + 1) // 2

            units = lax.fori_loop(0, at.half, row, units, unroll=4)
        for n in range(GROUP):
            out_ref[rows + units + n] = 0
            for k in range(2):
                out_ref[tiles + 2 * (units + n) + k] = 0
                out_ref[places + 2 * (units + n) + k] = zero
        out_ref[at.groups + side] = (units + GROUP - 1) // GROUP


def plan(columns, flags, blocks_all):
    slices, count = columns.shape
    size = Layout(slices, count // TPR).size
    return pl.pallas_call(
        functools.partial(plan_kernel, blocks_all),
        out_shape=pltpu.SMEM((size,), jnp.int32),
        in_specs=[SCALARS, SCALARS],
        out_specs=SCALARS,
        name="plan",
        compiler_params=pltpu.CompilerParams(vmem_limit_bytes=1 << 20),
    )(columns, flags)


def slice_ends(odd, left_ref, right_ref, near_ref, far_ref):
    half = left_ref.shape[2]
    last = left_ref.shape[0] - 1

    def fill(ref, s):
        ref[0, :, :half] = left_ref[s]
        ref[0, :, half:] = right_ref[s]

    @pl.when(odd == 0)
    def _():
        fill(near_ref, last)
        fill(far_ref, 0)

    @pl.when(odd != 0)
    def _():
        fill(near_ref, 0)
        fill(far_ref, last)


def start_kernel(odd_ref, x_ref, left_ref, right_ref, near_ref, far_ref):
    half = left_ref.shape[2]
    left_ref[...] = x_ref[:, :, :half]
    right_ref[...] = x_ref[:, :, half:]
    slice_ends(odd_ref[1], left_ref, right_ref, near_ref, far_ref)


def start(odd, block):
    slices, width, points = block.shape
    half = ((slices, width, points // 2), F32)
    whole = ((1, width, points), F32)
    return call(
        start_kernel,
        [odd, block],
        [half, half, whole, whole],
        specs=[SCALARS, WHOLE],
        moved=16 * block.size,
        name="start",
    )


def fold(product, width):
    return product[:width, :TILE] + product[:width, TILE:] + product[width:, :TILE]


def product(halves, tiles, width):
    left = jnp.concatenate(halves, axis=1)
    right = jnp.concatenate(tiles, axis=0)
    return fold(lax.dot_general(left, right, NN, preferred_element_type=F32), width)


def local_kernel(mode, scale, plan_ref, tiles_ref, *refs):
    y_refs, refs = refs[:2], refs[2:]
    previous_refs, (left_ref, right_ref, halves_ref) = refs[:-3], refs[-3:]
    slices, width, points = left_ref.shape
    half = points // TILE
    blocks = 2 * half
    at = Layout(slices, blocks)
    for s in range(slices):
        for b in range(blocks):
            k = b % half
            halves_ref[s * blocks + b] = stacked(y_refs[b // half][s, :, k * TILE : (k + 1) * TILE])
    halves_ref[slices * blocks] = jnp.zeros((2 * width, TILE), BF16)

    for s in range(slices):
        degree = 2.0
        if s == 0:
            degree = degree - jnp.where(plan_ref[at.flags + 2] != 0, 1.0, 0.0)
        if s == slices - 1:
            degree = degree - jnp.where(plan_ref[at.flags + 3] != 0, 1.0, 0.0)
        for side, out_ref in enumerate((left_ref, right_ref)):

            def row(k, carry, s=s, side=side, out_ref=out_ref, degree=degree):
                i = s * blocks + side * half + k
                halves = [halves_ref[plan_ref[i * TPR + n]] for n in range(TPR)]
                tiles = [tiles_ref[i * TPR + n] for n in range(TPR)]
                here = pl.ds(pl.multiple_of(k * TILE, TILE), TILE)
                y_ref = y_refs[side]
                y = y_ref[s, :, here]
                time = degree * y
                if s > 0:
                    time = time - y_ref[s - 1, :, here]
                if s < slices - 1:
                    time = time - y_ref[s + 1, :, here]
                image = product(halves, tiles, width) + INFLATION_FACTOR * time
                if mode != "image":
                    image = (image - CENTER * y) * scale
                if previous_refs:
                    image = image - previous_refs[side][s, :, here]
                out_ref[s, :, here] = image
                return carry

            lax.fori_loop(0, half, row, 0, unroll=8)


def local_part(mode, scale, table, tiles, ys, previous):
    slices, width, points = ys[0].shape
    rows = 2 * slices * points // TILE
    ins = [table, near(tiles)] + [near(y) for y in ys] + [near(y) for y in previous or ()]
    return call(
        functools.partial(local_kernel, mode, scale),
        ins,
        [(ys[0].shape, F32)] * 2,
        specs=[SCALARS] + [WHOLE] * (len(ins) - 1),
        scratch=[VM((rows + 1, 2 * width, TILE), BF16)],
        flops=2 * rows * TPR * 4 * width * TILE * TILE,
        moved=24 * ys[0].size,
        name="local_" + mode,
    )


def mix(matrix, y):
    high, low = split(matrix)
    y_high, y_low = split(y)
    left = jnp.concatenate([high, low, high], axis=1)
    right = jnp.concatenate([y_high, y_high, y_low], axis=0)
    return lax.dot_general(left, right, NN, preferred_element_type=F32)


def inner(left, right):
    width = left.shape[0]
    p = lax.dot_general(stacked(left), stacked(right), NT, preferred_element_type=F32)
    return (p[:width, :width] + p[width:, width:]) + (p[:width, width:] + p[width:, :width])


def side_kernel(side, second, mode, scale, plan_ref, tiles_ref, part_ref, halo_ref, near_ref, far_ref, *refs):
    refs = list(refs)
    halves_ref = refs.pop()
    slices, width, points = part_ref.shape
    half = points // TILE
    at = Layout(slices, 2 * half)
    inputs = 0
    if second:
        inputs = 4 if mode == "image" else 1
    given, (new_ref, *out_refs) = refs[:inputs], refs[inputs:]
    for s in range(slices):
        for b in range(HB):
            halves_ref[s * HB + b] = stacked(halo_ref[s, :, b * TILE : (b + 1) * TILE])
    halves_ref[slices * HB] = jnp.zeros((2 * width, TILE), BF16)

    here = slice(side * points, (side + 1) * points)
    time_odd = plan_ref[at.flags + 1] != 0
    factor = INFLATION_FACTOR * scale
    for s in range(slices):
        image = part_ref[s]
        if s == 0:
            before = jnp.where(time_odd, near_ref[0, :, here], far_ref[0, :, here])
            image = image - jnp.where(plan_ref[at.flags + 2] != 0, 0.0, factor * before)
        if s == slices - 1:
            after = jnp.where(time_odd, far_ref[0, :, here], near_ref[0, :, here])
            image = image - jnp.where(plan_ref[at.flags + 3] != 0, 0.0, factor * after)
        new_ref[s] = image

    rows = at.rows + side * at.room
    tiles_at = at.tiles + side * 2 * at.room
    places = at.places + side * 2 * at.room

    def group(g, carry):
        done = []
        for k in range(GROUP):
            u = g * GROUP + k
            halves = [halves_ref[plan_ref[places + 2 * u + j]] for j in range(2)]
            tiles = [tiles_ref[plan_ref[tiles_at + 2 * u + j]] for j in range(2)]
            done.append((plan_ref[rows + u], product(halves, tiles, width)))
        for i, value in done:
            to = pl.ds(pl.multiple_of((i % half) * TILE, TILE), TILE)
            new_ref[i // half, :, to] += scale * value
        return carry

    lax.fori_loop(0, plan_ref[at.groups + side], group, 0)

    pair = (lambda other: (new_ref, other)) if side == 0 else (lambda other: (other, new_ref))
    if second and mode == "image":
        image_ref, left_ref, right_ref, matrix_ref = given
        mixed_ref, gram_ref = out_refs
        matrix = matrix_ref[...]
        gram, product_sum = 0.0, 0.0
        images = pair(image_ref)
        for s in range(slices):
            for k, y_ref in enumerate((left_ref, right_ref)):
                mixed = mix(matrix, y_ref[s])
                mixed_ref[s, :, k * points : (k + 1) * points] = mixed
                gram = gram + inner(mixed, mixed)
                product_sum = product_sum + inner(mixed, mix(matrix, images[k][s]))
        gram_ref[...] = folded(gram, product_sum)
    elif second:
        slice_ends(plan_ref[at.flags + 1], *pair(given[0]), *out_refs[:2])
        out_refs = out_refs[2:]
        if mode == "gram":
            gram = sum(inner(y[s], y[s]) for y in (given[0], new_ref) for s in range(slices))
            gram_ref = out_refs.pop(0)
            gram_ref[...] = folded(gram)
    if mode != "image" and out_refs:
        side_points = HB * TILE
        start = points - side_points if side else 0
        out_refs[0][...] = new_ref[:, :, start : start + side_points]


def folded(*matrices):
    width = matrices[0].shape[0]
    rows = width * width * len(matrices) // TILE
    flat = jnp.concatenate(matrices, axis=0)
    return jnp.concatenate([flat[i : i + rows] for i in range(0, flat.shape[0], rows)], axis=1)


def unfolded(block, width):
    rows = block.shape[0]
    flat = jnp.concatenate([block[:, i : i + width] for i in range(0, TILE, width)], axis=0)
    return [flat[i : i + width] for i in range(0, flat.shape[0], width)]


def finish(side, second, mode, scale, table, tiles, part, halo, ends, given=()):
    slices, width, points = part.shape
    ins = [table] + [near(v) for v in (tiles, part, halo, *ends, *given)]
    outs = [(part.shape, F32)]
    whole = (slices, width, 2 * points)
    if second and mode == "image":
        outs += [(whole, F32), ((2 * width * width // TILE, TILE), F32)]
    elif second:
        outs += [((1, width, 2 * points), F32)] * 2
        if mode == "gram":
            outs.append(((width * width // TILE, TILE), F32))
    if mode != "image" and points != HB * TILE:
        outs.append(((slices, width, HB * TILE), F32))
    return call(
        functools.partial(side_kernel, side, second, mode, scale),
        ins,
        outs,
        scratch=[VM((slices * HB + 1, 2 * width, TILE), BF16)],
        specs=[SCALARS] + [WHOLE] * (len(ins) - 1),
        flops=2 * slices * points * 4 * width * TILE * 2,
        moved=24 * part.size,
        name=("left_", "right_")[side] + mode,
        aliases={2: 0},
    )


def inverse_factor(gram):
    width = gram.shape[0]
    square = (width, width)
    rows = lax.broadcasted_iota(jnp.int32, square, 0)
    columns = lax.broadcasted_iota(jnp.int32, square, 1)
    inverse = (rows == columns).astype(F32)
    column = jnp.broadcast_to(gram[:, :1], square)
    for j in range(width - 1):
        following = jnp.broadcast_to(gram[:, j + 1 : j + 2], square)
        scaled = jnp.where(rows > j, column, 0.0) * (1.0 / column[j : j + 1])
        gram = gram - scaled * gram[j : j + 1]
        inverse = inverse - scaled * inverse[j : j + 1]
        column = following - scaled * column[j + 1 : j + 2]
    pivots = jnp.sum(jnp.where(rows == columns, gram, 0.0), axis=1, keepdims=True)
    return inverse * lax.rsqrt(pivots)


def factor_kernel(count, gram_ref, out_ref):
    (gram,) = unfolded(gram_ref[...] * (1.0 / count), out_ref.shape[0])
    out_ref[...] = inverse_factor(gram)


def factor(gram, width, count):
    return call(
        functools.partial(factor_kernel, float(count)),
        [near(gram)],
        [((width, width), F32)],
        specs=[WHOLE],
        flops=40000 * gram.size,
        moved=8 * gram.size,
        name="factor",
    )[0]


def basis_kernel(matrix_ref, left_ref, right_ref, out_ref):
    half = left_ref.shape[2]
    for s in range(left_ref.shape[0]):
        out_ref[s, :, :half] = mix(matrix_ref[...], left_ref[s])
        out_ref[s, :, half:] = mix(matrix_ref[...], right_ref[s])


def basis(matrix, ys):
    slices, width, half = ys[0].shape
    return call(
        basis_kernel,
        [near(matrix)] + [near(y) for y in ys],
        [((slices, width, 2 * half), F32)],
        specs=[WHOLE] * 3,
        flops=4 * width * ys[0].size,
        moved=16 * ys[0].size,
        name="basis",
        out_vmem=False,
    )[0]


def close_kernel(count, sums_ref, y_ref, basis_ref, ritz_ref):
    high = lax.Precision.HIGHEST
    gram, projected = unfolded(sums_ref[...] * (1.0 / count), ritz_ref.shape[0])
    matrix = inverse_factor(gram)
    for s in range(y_ref.shape[0]):
        basis_ref[s] = mix(matrix, y_ref[s])
    half = lax.dot_general(matrix, projected, NN, precision=high, preferred_element_type=F32)
    ritz_ref[...] = lax.dot_general(half, matrix, NT, precision=high, preferred_element_type=F32)


def close(sums, y, count):
    width = y.shape[1]
    return call(
        functools.partial(close_kernel, float(count)),
        [near(sums), near(y)],
        [(y.shape, F32), ((width, width), F32)],
        specs=[WHOLE] * 2,
        flops=2 * width * y.size,
        moved=8 * y.size,
        name="close",
        out_vmem=False,
    )


def stages_of(axis):
    count = lax.axis_size(axis)
    found, stride = [], 1
    if (count.bit_length() - 1) % 2:
        found, stride = [(axis, (1,))], 2
    while stride < count:
        found.append((axis, (stride, 2 * stride, 3 * stride)))
        stride *= 4
    return found


def pairs_of(axis):
    return [(axis, (1 << k,)) for k in range((lax.axis_size(axis) - 1).bit_length())]


def add_over(value, stages):
    for axis, strides in stages:
        count = lax.axis_size(axis)
        others = [lax.ppermute(value, axis, [(i, i ^ k) for i in range(count)]) for k in strides]
        if len(others) == 1:
            value = value + others[0]
        else:
            value = (value + others[0]) + (others[1] + others[2])
    return value


def inner_pairs(axis):
    count = lax.axis_size(axis)
    return [(i, i ^ 1) for i in range(count)]


def outer_pairs(axis):
    count = lax.axis_size(axis)
    return [(i, (i + 1) % count if i % 2 else (i - 1) % count) for i in range(count)]


def body(start_block, stiffness_tiles, tile_columns):
    slices, width, local_points = start_block.shape
    local_blocks = local_points // TILE
    blocks_all = lax.axis_size("space") * local_blocks
    count_all = slices * local_points * lax.axis_size("tm") * lax.axis_size("space")
    time_index = lax.axis_index("tm")
    ends = (time_index == 0, time_index == lax.axis_size("tm") - 1)
    space_index = lax.axis_index("space")
    odd = jnp.stack(
        [
            space_index % 2,
            time_index % 2,
            ends[0].astype(jnp.int32),
            ends[1].astype(jnp.int32),
            space_index * local_blocks,
        ]
    )

    left, right, *ends = start(odd, start_block)
    side = HB * TILE
    half = left.shape[2]
    state = ((left, right), ends, (left[:, :, :side], right[:, :, half - side :]))
    table = plan(tile_columns, odd, blocks_all)
    tiles = prep(stiffness_tiles)

    across, along = pairs_of("space"), pairs_of("tm")
    early = [along[:-1], across[:1], across[1:], along[-1:]]
    ring = lax.axis_size("space")
    up = [(i, (i + 1) % ring) for i in range(ring)]
    down = [((i + 1) % ring, i) for i in range(ring)]

    def step(mode, scale, first, state, previous=None, beside=None):
        halves, ends, sides = state
        halos = [None, None]
        for side in (first, 1 - first):
            pairs = down if side == 1 else up
            halos[side] = lax.ppermute(sides[1 - side], "space", pairs)
        far_slice = lax.ppermute(ends[1], "tm", outer_pairs("tm"))
        near_slice = lax.ppermute(ends[0], "tm", inner_pairs("tm"))
        ends = (near_slice, far_slice)
        parts = local_part(mode, scale, table, tiles, halves, previous)
        extra = None
        if beside is not None:
            parts, extra = lax.optimization_barrier((parts, beside[0]))
            extra = beside[1](extra)
        news, sends = [None, None], [None, None]
        new, *own = finish(first, False, mode, scale, table, tiles, parts[first], halos[first], ends)
        news[first], sends[first] = new, own[0] if own else new
        given = (new, *halves, extra) if mode == "image" else (new,)
        last = 1 - first
        part, _ = lax.optimization_barrier((parts[last], halos[first]))
        if beside is not None:
            part, extra = lax.optimization_barrier((part, extra))
        new, *rest = finish(last, True, mode, scale, table, tiles, part, halos[last], ends, given)
        if mode == "image":
            return rest[0], rest[1], extra
        ends, rest = rest[:2], rest[2:]
        gram = rest.pop(0) if mode == "gram" else None
        news[last], sends[last] = new, rest[0] if rest else new
        return (tuple(news), ends, sends), gram, extra

    def stage(n):
        return lambda gram: add_over(gram, early[n])

    state0 = state
    state1, _, _ = step("first", 1.0 / RADIUS, 0, state0)
    state2, _, _ = step("step", 2.0 / RADIUS, 1, state1, state0[0])
    filtered, gram, _ = step("gram", 2.0 / RADIUS, 0, state2, state1[0])
    state1, _, gram = step("first", 1.0 / RADIUS, 1, filtered, None, (gram, stage(0)))
    state2, _, gram = step("step", 2.0 / RADIUS, 0, state1, filtered[0], (gram, stage(1)))
    state3, _, gram = step("step", 2.0 / RADIUS, 1, state2, state1[0], (gram, stage(2)))
    second, sums, matrix = step(
        "image", 1.0, 0, state3, None, (gram, lambda gram: factor(stage(3)(gram), width, count_all))
    )
    first_basis = basis(matrix, filtered[0])
    sums = add_over(sums, stages_of("tm") + stages_of("space"))
    ritz_basis, ritz_matrix = close(sums, second, count_all)
    return ritz_basis, first_basis, ritz_matrix


def solution(mesh):
    placed = (P("tm", None, "space"), P("tm", "space", None, None), P("tm", "space"))
    return jax.shard_map(
        body,
        mesh=mesh,
        in_specs=placed,
        out_specs=(P("tm", None, "space"), P("tm", None, "space"), P()),
        check_vma=False,
    )
```

```python
import functools

import jax
import jax.numpy as jnp
from jax import lax
from jax.experimental import pallas as pl
from jax.experimental.pallas import tpu as pltpu
from jax.sharding import PartitionSpec as P

TILE = 128
TPR = 5
HB = 8
CENTER = 6.5
RADIUS = 3.5
INFLATION_FACTOR = 0.8
GROUP = 8

F32 = jnp.float32
BF16 = jnp.bfloat16
VM = pltpu.VMEM
NT = (((1,), (1,)), ((), ()))
NN = (((1,), (0,)), ((), ()))
WHOLE = pl.BlockSpec(memory_space=VM)
SCALARS = pl.BlockSpec(memory_space=pltpu.SMEM)


def near(x):
    return pltpu.with_memory_space_constraint(x, VM)


def split(x):
    high = x.astype(BF16)
    return high, (x - high.astype(F32)).astype(BF16)


def stacked(x):
    return jnp.concatenate(split(x), axis=0)


def call(kernel, ins, outs, scratch=(), specs=None, flops=0, moved=0, name=None, out_vmem=True, aliases=None):
    out_shape = [VM(s, d) if out_vmem else jax.ShapeDtypeStruct(s, d) for s, d in outs]
    return pl.pallas_call(
        kernel,
        out_shape=out_shape,
        in_specs=specs,
        out_specs=[WHOLE] * len(outs),
        scratch_shapes=list(scratch),
        name=name,
        input_output_aliases=aliases or {},
        cost_estimate=pl.CostEstimate(flops=flops, bytes_accessed=moved, transcendentals=0),
        compiler_params=pltpu.CompilerParams(vmem_limit_bytes=6 << 20),
    )(*ins)


def prep_kernel(tiles_ref, out_ref, buffer_ref, semaphores):
    slots, step = buffer_ref.shape[:2]
    chunks = tiles_ref.shape[0] // step

    def copy(c):
        slot = lax.rem(c, slots)
        return pltpu.make_async_copy(
            tiles_ref.at[pl.ds(c * step, step)], buffer_ref.at[slot], semaphores.at[slot]
        )

    for c in range(slots):
        copy(c).start()

    def chunk(c, carry):
        copy(c).wait()
        slot = lax.rem(c, slots)
        for n in range(step):
            high, low = split(buffer_ref[slot, n].T)
            out_ref[c * step + n, :, :TILE] = high
            out_ref[c * step + n, :, TILE:] = low

        @pl.when(c + slots < chunks)
        def _():
            copy(c + slots).start()

        return carry

    lax.fori_loop(0, chunks, chunk, 0)


def prep(tiles):
    tiles = tiles.reshape(-1, TILE, TILE)
    slots, step = 5, 16
    return pl.pallas_call(
        prep_kernel,
        out_shape=VM((tiles.shape[0], TILE, 2 * TILE), BF16),
        in_specs=[pl.BlockSpec(memory_space=pltpu.HBM)],
        out_specs=WHOLE,
        scratch_shapes=[VM((slots, step, TILE, TILE), F32), pltpu.SemaphoreType.DMA((slots,))],
        name="prep",
        cost_estimate=pl.CostEstimate(flops=0, bytes_accessed=4 * tiles.size, transcendentals=0),
        compiler_params=pltpu.CompilerParams(vmem_limit_bytes=8 << 20),
    )(pltpu.with_memory_space_constraint(tiles, pltpu.HBM))


class Layout:
    def __init__(self, slices, blocks):
        self.half = blocks // 2
        self.room = slices * self.half * (TPR // 2) + GROUP + 2
        self.rows = slices * blocks * TPR
        self.tiles = self.rows + 2 * self.room
        self.places = self.tiles + 4 * self.room
        self.groups = self.places + 4 * self.room
        self.flags = self.groups + 2
        self.size = -(-(self.flags + 4) // 128) * 128


def plan_kernel(blocks_all, columns_ref, flags_ref, out_ref):
    slices, count = columns_ref.shape
    blocks = count // TPR
    at = Layout(slices, blocks)
    for i in range(4):
        out_ref[at.flags + i] = flags_ref[i]
    first_block = flags_ref[4]
    here = slices * blocks
    zero = slices * HB
    for side in range(2):
        rows = at.rows + side * at.room
        tiles = at.tiles + side * 2 * at.room
        places = at.places + side * 2 * at.room
        units = jnp.int32(0)
        for s in range(slices):

            def row(k, units, s=s, side=side, rows=rows, tiles=tiles, places=places):
                r = side * at.half + k
                i = s * blocks + r
                out_ref[rows + units] = s * at.half + k
                out_ref[rows + units + 1] = s * at.half + k
                found = jnp.int32(0)
                for n in range(TPR):
                    where = columns_ref[s, r * TPR + n] - first_block + HB
                    where = jnp.where(where < 0, where + blocks_all, where)
                    where = jnp.where(where >= blocks_all, where - blocks_all, where)
                    away = where >= HB + blocks if side else where < HB
                    out_ref[i * TPR + n] = jnp.where(away, here, s * blocks + where - HB)
                    if n > 0:
                        out_ref[tiles + 2 * units + found] = i * TPR + n
                        out_ref[places + 2 * units + found] = s * HB + where - side * (HB + blocks)
                        found = found + away.astype(jnp.int32)
                out_ref[tiles + 2 * units + found] = i * TPR
                out_ref[places + 2 * units + found] = zero
                return units + (found + 1) // 2

            units = lax.fori_loop(0, at.half, row, units, unroll=4)
        for n in range(GROUP):
            out_ref[rows + units + n] = 0
            for k in range(2):
                out_ref[tiles + 2 * (units + n) + k] = 0
                out_ref[places + 2 * (units + n) + k] = zero
        out_ref[at.groups + side] = (units + GROUP - 1) // GROUP


def plan(columns, flags, blocks_all):
    slices, count = columns.shape
    size = Layout(slices, count // TPR).size
    return pl.pallas_call(
        functools.partial(plan_kernel, blocks_all),
        out_shape=pltpu.SMEM((size,), jnp.int32),
        in_specs=[SCALARS, SCALARS],
        out_specs=SCALARS,
        name="plan",
        compiler_params=pltpu.CompilerParams(vmem_limit_bytes=1 << 20),
    )(columns, flags)


def slice_ends(odd, left_ref, right_ref, near_ref, far_ref):
    half = left_ref.shape[2]
    last = left_ref.shape[0] - 1

    def fill(ref, s):
        ref[0, :, :half] = left_ref[s]
        ref[0, :, half:] = right_ref[s]

    @pl.when(odd == 0)
    def _():
        fill(near_ref, last)
        fill(far_ref, 0)

    @pl.when(odd != 0)
    def _():
        fill(near_ref, 0)
        fill(far_ref, last)


def start_kernel(odd_ref, x_ref, left_ref, right_ref, near_ref, far_ref):
    half = left_ref.shape[2]
    left_ref[...] = x_ref[:, :, :half]
    right_ref[...] = x_ref[:, :, half:]
    slice_ends(odd_ref[1], left_ref, right_ref, near_ref, far_ref)


def start(odd, block):
    slices, width, points = block.shape
    half = ((slices, width, points // 2), F32)
    whole = ((1, width, points), F32)
    return call(
        start_kernel,
        [odd, block],
        [half, half, whole, whole],
        specs=[SCALARS, WHOLE],
        moved=16 * block.size,
        name="start",
    )


def fold(product, width):
    return product[:width, :TILE] + product[:width, TILE:] + product[width:, :TILE]


def product(halves, tiles, width):
    left = jnp.concatenate(halves, axis=1)
    right = jnp.concatenate(tiles, axis=0)
    return fold(lax.dot_general(left, right, NN, preferred_element_type=F32), width)


def local_kernel(mode, scale, plan_ref, tiles_ref, *refs):
    y_refs, refs = refs[:2], refs[2:]
    previous_refs, (left_ref, right_ref, halves_ref) = refs[:-3], refs[-3:]
    slices, width, points = left_ref.shape
    half = points // TILE
    blocks = 2 * half
    at = Layout(slices, blocks)
    for s in range(slices):
        for b in range(blocks):
            k = b % half
            halves_ref[s * blocks + b] = stacked(y_refs[b // half][s, :, k * TILE : (k + 1) * TILE])
    halves_ref[slices * blocks] = jnp.zeros((2 * width, TILE), BF16)

    for s in range(slices):
        degree = 2.0
        if s == 0:
            degree = degree - jnp.where(plan_ref[at.flags + 2] != 0, 1.0, 0.0)
        if s == slices - 1:
            degree = degree - jnp.where(plan_ref[at.flags + 3] != 0, 1.0, 0.0)
        for side, out_ref in enumerate((left_ref, right_ref)):

            def row(k, carry, s=s, side=side, out_ref=out_ref, degree=degree):
                i = s * blocks + side * half + k
                halves = [halves_ref[plan_ref[i * TPR + n]] for n in range(TPR)]
                tiles = [tiles_ref[i * TPR + n] for n in range(TPR)]
                here = pl.ds(pl.multiple_of(k * TILE, TILE), TILE)
                y_ref = y_refs[side]
                y = y_ref[s, :, here]
                time = degree * y
                if s > 0:
                    time = time - y_ref[s - 1, :, here]
                if s < slices - 1:
                    time = time - y_ref[s + 1, :, here]
                image = product(halves, tiles, width) + INFLATION_FACTOR * time
                if mode != "image":
                    image = (image - CENTER * y) * scale
                if previous_refs:
                    image = image - previous_refs[side][s, :, here]
                out_ref[s, :, here] = image
                return carry

            lax.fori_loop(0, half, row, 0, unroll=8)


def local_part(mode, scale, table, tiles, ys, previous):
    slices, width, points = ys[0].shape
    rows = 2 * slices * points // TILE
    ins = [table, near(tiles)] + [near(y) for y in ys] + [near(y) for y in previous or ()]
    return call(
        functools.partial(local_kernel, mode, scale),
        ins,
        [(ys[0].shape, F32)] * 2,
        specs=[SCALARS] + [WHOLE] * (len(ins) - 1),
        scratch=[VM((rows + 1, 2 * width, TILE), BF16)],
        flops=2 * rows * TPR * 4 * width * TILE * TILE,
        moved=24 * ys[0].size,
        name="local_" + mode,
    )


def mix(matrix, y):
    high, low = split(matrix)
    y_high, y_low = split(y)
    left = jnp.concatenate([high, low, high], axis=1)
    right = jnp.concatenate([y_high, y_high, y_low], axis=0)
    return lax.dot_general(left, right, NN, preferred_element_type=F32)


def inner(left, right):
    width = left.shape[0]
    p = lax.dot_general(stacked(left), stacked(right), NT, preferred_element_type=F32)
    return (p[:width, :width] + p[width:, width:]) + (p[:width, width:] + p[width:, :width])


def side_kernel(side, second, mode, scale, plan_ref, tiles_ref, part_ref, halo_ref, near_ref, far_ref, *refs):
    refs = list(refs)
    halves_ref = refs.pop()
    slices, width, points = part_ref.shape
    half = points // TILE
    at = Layout(slices, 2 * half)
    inputs = 0
    if second:
        inputs = 4 if mode == "image" else 1
    given, (new_ref, *out_refs) = refs[:inputs], refs[inputs:]
    for s in range(slices):
        for b in range(HB):
            halves_ref[s * HB + b] = stacked(halo_ref[s, :, b * TILE : (b + 1) * TILE])
    halves_ref[slices * HB] = jnp.zeros((2 * width, TILE), BF16)

    here = slice(side * points, (side + 1) * points)
    time_odd = plan_ref[at.flags + 1] != 0
    factor = INFLATION_FACTOR * scale
    for s in range(slices):
        image = part_ref[s]
        if s == 0:
            before = jnp.where(time_odd, near_ref[0, :, here], far_ref[0, :, here])
            image = image - jnp.where(plan_ref[at.flags + 2] != 0, 0.0, factor * before)
        if s == slices - 1:
            after = jnp.where(time_odd, far_ref[0, :, here], near_ref[0, :, here])
            image = image - jnp.where(plan_ref[at.flags + 3] != 0, 0.0, factor * after)
        new_ref[s] = image

    rows = at.rows + side * at.room
    tiles_at = at.tiles + side * 2 * at.room
    places = at.places + side * 2 * at.room

    def group(g, carry):
        done = []
        for k in range(GROUP):
            u = g * GROUP + k
            halves = [halves_ref[plan_ref[places + 2 * u + j]] for j in range(2)]
            tiles = [tiles_ref[plan_ref[tiles_at + 2 * u + j]] for j in range(2)]
            done.append((plan_ref[rows + u], product(halves, tiles, width)))
        for i, value in done:
            to = pl.ds(pl.multiple_of((i % half) * TILE, TILE), TILE)
            new_ref[i // half, :, to] += scale * value
        return carry

    lax.fori_loop(0, plan_ref[at.groups + side], group, 0)

    pair = (lambda other: (new_ref, other)) if side == 0 else (lambda other: (other, new_ref))
    if second and mode == "image":
        image_ref, left_ref, right_ref, matrix_ref = given
        mixed_ref, gram_ref = out_refs
        matrix = matrix_ref[...]
        gram, product_sum = 0.0, 0.0
        images = pair(image_ref)
        for s in range(slices):
            for k, y_ref in enumerate((left_ref, right_ref)):
                mixed = mix(matrix, y_ref[s])
                mixed_ref[s, :, k * points : (k + 1) * points] = mixed
                gram = gram + inner(mixed, mixed)
                product_sum = product_sum + inner(mixed, mix(matrix, images[k][s]))
        gram_ref[...] = folded(gram, product_sum)
    elif second:
        slice_ends(plan_ref[at.flags + 1], *pair(given[0]), *out_refs[:2])
        out_refs = out_refs[2:]
        if mode == "gram":
            gram = sum(inner(y[s], y[s]) for y in (given[0], new_ref) for s in range(slices))
            gram_ref = out_refs.pop(0)
            gram_ref[...] = folded(gram)
    if mode != "image" and out_refs:
        side_points = HB * TILE
        start = points - side_points if side else 0
        out_refs[0][...] = new_ref[:, :, start : start + side_points]


def folded(*matrices):
    width = matrices[0].shape[0]
    rows = width * width * len(matrices) // TILE
    flat = jnp.concatenate(matrices, axis=0)
    return jnp.concatenate([flat[i : i + rows] for i in range(0, flat.shape[0], rows)], axis=1)


def unfolded(block, width):
    rows = block.shape[0]
    flat = jnp.concatenate([block[:, i : i + width] for i in range(0, TILE, width)], axis=0)
    return [flat[i : i + width] for i in range(0, flat.shape[0], width)]


def finish(side, second, mode, scale, table, tiles, part, halo, ends, given=()):
    slices, width, points = part.shape
    ins = [table] + [near(v) for v in (tiles, part, halo, *ends, *given)]
    outs = [(part.shape, F32)]
    whole = (slices, width, 2 * points)
    if second and mode == "image":
        outs += [(whole, F32), ((2 * width * width // TILE, TILE), F32)]
    elif second:
        outs += [((1, width, 2 * points), F32)] * 2
        if mode == "gram":
            outs.append(((width * width // TILE, TILE), F32))
    if mode != "image" and points != HB * TILE:
        outs.append(((slices, width, HB * TILE), F32))
    return call(
        functools.partial(side_kernel, side, second, mode, scale),
        ins,
        outs,
        scratch=[VM((slices * HB + 1, 2 * width, TILE), BF16)],
        specs=[SCALARS] + [WHOLE] * (len(ins) - 1),
        flops=2 * slices * points * 4 * width * TILE * 2,
        moved=24 * part.size,
        name=("left_", "right_")[side] + mode,
        aliases={2: 0},
    )


def inverse_factor(gram):
    width = gram.shape[0]
    square = (width, width)
    rows = lax.broadcasted_iota(jnp.int32, square, 0)
    columns = lax.broadcasted_iota(jnp.int32, square, 1)
    inverse = (rows == columns).astype(F32)
    column = jnp.broadcast_to(gram[:, :1], square)
    for j in range(width - 1):
        following = jnp.broadcast_to(gram[:, j + 1 : j + 2], square)
        scaled = jnp.where(rows > j, column, 0.0) * (1.0 / column[j : j + 1])
        gram = gram - scaled * gram[j : j + 1]
        inverse = inverse - scaled * inverse[j : j + 1]
        column = following - scaled * column[j + 1 : j + 2]
    pivots = jnp.sum(jnp.where(rows == columns, gram, 0.0), axis=1, keepdims=True)
    return inverse * lax.rsqrt(pivots)


def factor_kernel(count, gram_ref, out_ref):
    (gram,) = unfolded(gram_ref[...] * (1.0 / count), out_ref.shape[0])
    out_ref[...] = inverse_factor(gram)


def factor(gram, width, count):
    return call(
        functools.partial(factor_kernel, float(count)),
        [near(gram)],
        [((width, width), F32)],
        specs=[WHOLE],
        flops=40000 * gram.size,
        moved=8 * gram.size,
        name="factor",
    )[0]


def basis_kernel(matrix_ref, left_ref, right_ref, out_ref):
    half = left_ref.shape[2]
    for s in range(left_ref.shape[0]):
        out_ref[s, :, :half] = mix(matrix_ref[...], left_ref[s])
        out_ref[s, :, half:] = mix(matrix_ref[...], right_ref[s])


def basis(matrix, ys):
    slices, width, half = ys[0].shape
    return call(
        basis_kernel,
        [near(matrix)] + [near(y) for y in ys],
        [((slices, width, 2 * half), F32)],
        specs=[WHOLE] * 3,
        flops=4 * width * ys[0].size,
        moved=16 * ys[0].size,
        name="basis",
        out_vmem=False,
    )[0]


def close_kernel(count, sums_ref, y_ref, basis_ref, ritz_ref):
    high = lax.Precision.HIGHEST
    gram, projected = unfolded(sums_ref[...] * (1.0 / count), ritz_ref.shape[0])
    matrix = inverse_factor(gram)
    for s in range(y_ref.shape[0]):
        basis_ref[s] = mix(matrix, y_ref[s])
    half = lax.dot_general(matrix, projected, NN, precision=high, preferred_element_type=F32)
    ritz_ref[...] = lax.dot_general(half, matrix, NT, precision=high, preferred_element_type=F32)


def close(sums, y, count):
    width = y.shape[1]
    return call(
        functools.partial(close_kernel, float(count)),
        [near(sums), near(y)],
        [(y.shape, F32), ((width, width), F32)],
        specs=[WHOLE] * 2,
        flops=2 * width * y.size,
        moved=8 * y.size,
        name="close",
        out_vmem=False,
    )


def stages_of(axis):
    count = lax.axis_size(axis)
    found, stride = [], 1
    if (count.bit_length() - 1) % 2:
        found, stride = [(axis, (1,))], 2
    while stride < count:
        found.append((axis, (stride, 2 * stride, 3 * stride)))
        stride *= 4
    return found


def pairs_of(axis):
    return [(axis, (1 << k,)) for k in range((lax.axis_size(axis) - 1).bit_length())]


def add_over(value, stages):
    for axis, strides in stages:
        count = lax.axis_size(axis)
        others = [lax.ppermute(value, axis, [(i, i ^ k) for i in range(count)]) for k in strides]
        if len(others) == 1:
            value = value + others[0]
        else:
            value = (value + others[0]) + (others[1] + others[2])
    return value


def inner_pairs(axis):
    count = lax.axis_size(axis)
    return [(i, i ^ 1) for i in range(count)]


def outer_pairs(axis):
    count = lax.axis_size(axis)
    return [(i, (i + 1) % count if i % 2 else (i - 1) % count) for i in range(count)]


def body(start_block, stiffness_tiles, tile_columns):
    slices, width, local_points = start_block.shape
    local_blocks = local_points // TILE
    blocks_all = lax.axis_size("space") * local_blocks
    count_all = slices * local_points * lax.axis_size("tm") * lax.axis_size("space")
    time_index = lax.axis_index("tm")
    ends = (time_index == 0, time_index == lax.axis_size("tm") - 1)
    space_index = lax.axis_index("space")
    odd = jnp.stack(
        [
            space_index % 2,
            time_index % 2,
            ends[0].astype(jnp.int32),
            ends[1].astype(jnp.int32),
            space_index * local_blocks,
        ]
    )

    left, right, *ends = start(odd, start_block)
    side = HB * TILE
    half = left.shape[2]
    state = ((left, right), ends, (left[:, :, :side], right[:, :, half - side :]))
    table = plan(tile_columns, odd, blocks_all)
    tiles = prep(stiffness_tiles)

    across, along = pairs_of("space"), pairs_of("tm")
    early = [along[:-1], along[-1:], across[:1], across[1:]]
    ring = lax.axis_size("space")
    up = [(i, (i + 1) % ring) for i in range(ring)]
    down = [((i + 1) % ring, i) for i in range(ring)]

    def step(mode, scale, first, state, previous=None, beside=None):
        halves, ends, sides = state
        halos = [None, None]
        for side in (first, 1 - first):
            pairs = down if side == 1 else up
            halos[side] = lax.ppermute(sides[1 - side], "space", pairs)
        far_slice = lax.ppermute(ends[1], "tm", outer_pairs("tm"))
        near_slice = lax.ppermute(ends[0], "tm", inner_pairs("tm"))
        ends = (near_slice, far_slice)
        parts = local_part(mode, scale, table, tiles, halves, previous)
        extra = None
        if beside is not None:
            parts, extra = lax.optimization_barrier((parts, beside[0]))
            extra = beside[1](extra)
        news, sends = [None, None], [None, None]
        new, *own = finish(first, False, mode, scale, table, tiles, parts[first], halos[first], ends)
        news[first], sends[first] = new, own[0] if own else new
        given = (new, *halves, extra) if mode == "image" else (new,)
        last = 1 - first
        part, _ = lax.optimization_barrier((parts[last], halos[first]))
        if beside is not None:
            part, extra = lax.optimization_barrier((part, extra))
        new, *rest = finish(last, True, mode, scale, table, tiles, part, halos[last], ends, given)
        if mode == "image":
            return rest[0], rest[1], extra
        ends, rest = rest[:2], rest[2:]
        gram = rest.pop(0) if mode == "gram" else None
        news[last], sends[last] = new, rest[0] if rest else new
        return (tuple(news), ends, sends), gram, extra

    def stage(n):
        return lambda gram: add_over(gram, early[n])

    state0 = state
    state1, _, _ = step("first", 1.0 / RADIUS, 0, state0)
    state2, _, _ = step("step", 2.0 / RADIUS, 1, state1, state0[0])
    filtered, gram, _ = step("gram", 2.0 / RADIUS, 0, state2, state1[0])
    state1, _, gram = step("first", 1.0 / RADIUS, 1, filtered, None, (gram, stage(0)))
    state2, _, gram = step("step", 2.0 / RADIUS, 0, state1, filtered[0], (gram, stage(1)))
    state3, _, gram = step("step", 2.0 / RADIUS, 1, state2, state1[0], (gram, stage(2)))
    second, sums, matrix = step(
        "image", 1.0, 0, state3, None, (gram, lambda gram: factor(stage(3)(gram), width, count_all))
    )
    first_basis = basis(matrix, filtered[0])
    sums = add_over(sums, stages_of("tm") + stages_of("space"))
    ritz_basis, ritz_matrix = close(sums, second, count_all)
    return ritz_basis, first_basis, ritz_matrix


def solution(mesh):
    placed = (P("tm", None, "space"), P("tm", "space", None, None), P("tm", "space"))
    return jax.shard_map(
        body,
        mesh=mesh,
        in_specs=placed,
        out_specs=(P("tm", None, "space"), P("tm", None, "space"), P()),
        check_vma=False,
    )
```

```python
import functools

import jax
import jax.numpy as jnp
from jax import lax
from jax.experimental import pallas as pl
from jax.experimental.pallas import tpu as pltpu
from jax.sharding import PartitionSpec as P

TILE = 128
TPR = 5
HB = 8
CENTER = 6.5
RADIUS = 3.5
INFLATION_FACTOR = 0.8
GROUP = 8

F32 = jnp.float32
BF16 = jnp.bfloat16
VM = pltpu.VMEM
NT = (((1,), (1,)), ((), ()))
NN = (((1,), (0,)), ((), ()))
WHOLE = pl.BlockSpec(memory_space=VM)
SCALARS = pl.BlockSpec(memory_space=pltpu.SMEM)


def near(x):
    return pltpu.with_memory_space_constraint(x, VM)


def split(x):
    high = x.astype(BF16)
    return high, (x - high.astype(F32)).astype(BF16)


def stacked(x):
    return jnp.concatenate(split(x), axis=0)


def call(kernel, ins, outs, scratch=(), specs=None, flops=0, moved=0, name=None, out_vmem=True, aliases=None):
    out_shape = [VM(s, d) if out_vmem else jax.ShapeDtypeStruct(s, d) for s, d in outs]
    return pl.pallas_call(
        kernel,
        out_shape=out_shape,
        in_specs=specs,
        out_specs=[WHOLE] * len(outs),
        scratch_shapes=list(scratch),
        name=name,
        input_output_aliases=aliases or {},
        cost_estimate=pl.CostEstimate(flops=flops, bytes_accessed=moved, transcendentals=0),
        compiler_params=pltpu.CompilerParams(vmem_limit_bytes=6 << 20),
    )(*ins)


def prep_kernel(tiles_ref, out_ref, buffer_ref, semaphores):
    slots, step = buffer_ref.shape[:2]
    chunks = tiles_ref.shape[0] // step

    def copy(c):
        slot = lax.rem(c, slots)
        return pltpu.make_async_copy(
            tiles_ref.at[pl.ds(c * step, step)], buffer_ref.at[slot], semaphores.at[slot]
        )

    for c in range(slots):
        copy(c).start()

    def chunk(c, carry):
        copy(c).wait()
        slot = lax.rem(c, slots)
        for n in range(step):
            high, low = split(buffer_ref[slot, n])
            out_ref[c * step + n, :, :TILE] = high.T
            out_ref[c * step + n, :, TILE:] = low.T

        @pl.when(c + slots < chunks)
        def _():
            copy(c + slots).start()

        return carry

    lax.fori_loop(0, chunks, chunk, 0)


def prep(tiles):
    tiles = tiles.reshape(-1, TILE, TILE)
    slots, step = 5, 16
    return pl.pallas_call(
        prep_kernel,
        out_shape=VM((tiles.shape[0], TILE, 2 * TILE), BF16),
        in_specs=[pl.BlockSpec(memory_space=pltpu.HBM)],
        out_specs=WHOLE,
        scratch_shapes=[VM((slots, step, TILE, TILE), F32), pltpu.SemaphoreType.DMA((slots,))],
        name="prep",
        cost_estimate=pl.CostEstimate(flops=0, bytes_accessed=4 * tiles.size, transcendentals=0),
        compiler_params=pltpu.CompilerParams(vmem_limit_bytes=8 << 20),
    )(pltpu.with_memory_space_constraint(tiles, pltpu.HBM))


class Layout:
    def __init__(self, slices, blocks):
        self.half = blocks // 2
        self.room = slices * self.half * (TPR // 2) + GROUP + 2
        self.rows = slices * blocks * TPR
        self.tiles = self.rows + 2 * self.room
        self.places = self.tiles + 4 * self.room
        self.groups = self.places + 4 * self.room
        self.flags = self.groups + 2
        self.size = -(-(self.flags + 4) // 128) * 128


def plan_kernel(blocks_all, columns_ref, flags_ref, out_ref):
    slices, count = columns_ref.shape
    blocks = count // TPR
    at = Layout(slices, blocks)
    for i in range(4):
        out_ref[at.flags + i] = flags_ref[i]
    first_block = flags_ref[4]
    here = slices * blocks
    zero = slices * HB
    for side in range(2):
        rows = at.rows + side * at.room
        tiles = at.tiles + side * 2 * at.room
        places = at.places + side * 2 * at.room
        units = jnp.int32(0)
        for s in range(slices):

            def row(k, units, s=s, side=side, rows=rows, tiles=tiles, places=places):
                r = side * at.half + k
                i = s * blocks + r
                out_ref[rows + units] = s * at.half + k
                out_ref[rows + units + 1] = s * at.half + k
                found = jnp.int32(0)
                for n in range(TPR):
                    where = columns_ref[s, r * TPR + n] - first_block + HB
                    where = jnp.where(where < 0, where + blocks_all, where)
                    where = jnp.where(where >= blocks_all, where - blocks_all, where)
                    away = where >= HB + blocks if side else where < HB
                    out_ref[i * TPR + n] = jnp.where(away, here, s * blocks + where - HB)
                    if n > 0:
                        out_ref[tiles + 2 * units + found] = i * TPR + n
                        out_ref[places + 2 * units + found] = s * HB + where - side * (HB + blocks)
                        found = found + away.astype(jnp.int32)
                out_ref[tiles + 2 * units + found] = i * TPR
                out_ref[places + 2 * units + found] = zero
                return units + (found + 1) // 2

            units = lax.fori_loop(0, at.half, row, units, unroll=4)
        for n in range(GROUP):
            out_ref[rows + units + n] = 0
            for k in range(2):
                out_ref[tiles + 2 * (units + n) + k] = 0
                out_ref[places + 2 * (units + n) + k] = zero
        out_ref[at.groups + side] = (units + GROUP - 1) // GROUP


def plan(columns, flags, blocks_all):
    slices, count = columns.shape
    size = Layout(slices, count // TPR).size
    return pl.pallas_call(
        functools.partial(plan_kernel, blocks_all),
        out_shape=pltpu.SMEM((size,), jnp.int32),
        in_specs=[SCALARS, SCALARS],
        out_specs=SCALARS,
        name="plan",
        compiler_params=pltpu.CompilerParams(vmem_limit_bytes=1 << 20),
    )(columns, flags)


def slice_ends(odd, left_ref, right_ref, near_ref, far_ref):
    half = left_ref.shape[2]
    last = left_ref.shape[0] - 1

    def fill(ref, s):
        ref[0, :, :half] = left_ref[s]
        ref[0, :, half:] = right_ref[s]

    @pl.when(odd == 0)
    def _():
        fill(near_ref, last)
        fill(far_ref, 0)

    @pl.when(odd != 0)
    def _():
        fill(near_ref, 0)
        fill(far_ref, last)


def start_kernel(odd_ref, x_ref, left_ref, right_ref, near_ref, far_ref):
    half = left_ref.shape[2]
    left_ref[...] = x_ref[:, :, :half]
    right_ref[...] = x_ref[:, :, half:]
    slice_ends(odd_ref[1], left_ref, right_ref, near_ref, far_ref)


def start(odd, block):
    slices, width, points = block.shape
    half = ((slices, width, points // 2), F32)
    whole = ((1, width, points), F32)
    return call(
        start_kernel,
        [odd, block],
        [half, half, whole, whole],
        specs=[SCALARS, WHOLE],
        moved=16 * block.size,
        name="start",
    )


def fold(product, width):
    return product[:width, :TILE] + product[:width, TILE:] + product[width:, :TILE]


def product(halves, tiles, width):
    left = jnp.concatenate(halves, axis=1)
    right = jnp.concatenate(tiles, axis=0)
    return fold(lax.dot_general(left, right, NN, preferred_element_type=F32), width)


def local_kernel(mode, scale, plan_ref, tiles_ref, *refs):
    y_refs, refs = refs[:2], refs[2:]
    previous_refs, (left_ref, right_ref, halves_ref) = refs[:-3], refs[-3:]
    slices, width, points = left_ref.shape
    half = points // TILE
    blocks = 2 * half
    at = Layout(slices, blocks)
    for s in range(slices):
        for b in range(blocks):
            k = b % half
            halves_ref[s * blocks + b] = stacked(y_refs[b // half][s, :, k * TILE : (k + 1) * TILE])
    halves_ref[slices * blocks] = jnp.zeros((2 * width, TILE), BF16)

    for s in range(slices):
        degree = 2.0
        if s == 0:
            degree = degree - jnp.where(plan_ref[at.flags + 2] != 0, 1.0, 0.0)
        if s == slices - 1:
            degree = degree - jnp.where(plan_ref[at.flags + 3] != 0, 1.0, 0.0)
        for side, out_ref in enumerate((left_ref, right_ref)):

            def row(k, carry, s=s, side=side, out_ref=out_ref, degree=degree):
                i = s * blocks + side * half + k
                halves = [halves_ref[plan_ref[i * TPR + n]] for n in range(TPR)]
                tiles = [tiles_ref[i * TPR + n] for n in range(TPR)]
                here = pl.ds(pl.multiple_of(k * TILE, TILE), TILE)
                y_ref = y_refs[side]
                y = y_ref[s, :, here]
                time = degree * y
                if s > 0:
                    time = time - y_ref[s - 1, :, here]
                if s < slices - 1:
                    time = time - y_ref[s + 1, :, here]
                image = product(halves, tiles, width) + INFLATION_FACTOR * time
                if mode != "image":
                    image = (image - CENTER * y) * scale
                if previous_refs:
                    image = image - previous_refs[side][s, :, here]
                out_ref[s, :, here] = image
                return carry

            lax.fori_loop(0, half, row, 0, unroll=8)


def local_part(mode, scale, table, tiles, ys, previous):
    slices, width, points = ys[0].shape
    rows = 2 * slices * points // TILE
    ins = [table, near(tiles)] + [near(y) for y in ys] + [near(y) for y in previous or ()]
    return call(
        functools.partial(local_kernel, mode, scale),
        ins,
        [(ys[0].shape, F32)] * 2,
        specs=[SCALARS] + [WHOLE] * (len(ins) - 1),
        scratch=[VM((rows + 1, 2 * width, TILE), BF16)],
        flops=2 * rows * TPR * 4 * width * TILE * TILE,
        moved=24 * ys[0].size,
        name="local_" + mode,
    )


def mix(matrix, y):
    high, low = split(matrix)
    y_high, y_low = split(y)
    left = jnp.concatenate([high, low, high], axis=1)
    right = jnp.concatenate([y_high, y_high, y_low], axis=0)
    return lax.dot_general(left, right, NN, preferred_element_type=F32)


def inner(left, right):
    width = left.shape[0]
    p = lax.dot_general(stacked(left), stacked(right), NT, preferred_element_type=F32)
    return (p[:width, :width] + p[width:, width:]) + (p[:width, width:] + p[width:, :width])


def side_kernel(side, second, mode, scale, plan_ref, tiles_ref, part_ref, halo_ref, near_ref, far_ref, *refs):
    refs = list(refs)
    halves_ref = refs.pop()
    slices, width, points = part_ref.shape
    half = points // TILE
    at = Layout(slices, 2 * half)
    inputs = 0
    if second:
        inputs = 4 if mode == "image" else 1
    given, (new_ref, *out_refs) = refs[:inputs], refs[inputs:]
    for s in range(slices):
        for b in range(HB):
            halves_ref[s * HB + b] = stacked(halo_ref[s, :, b * TILE : (b + 1) * TILE])
    halves_ref[slices * HB] = jnp.zeros((2 * width, TILE), BF16)

    here = slice(side * points, (side + 1) * points)
    time_odd = plan_ref[at.flags + 1] != 0
    factor = INFLATION_FACTOR * scale
    for s in range(slices):
        image = part_ref[s]
        if s == 0:
            before = jnp.where(time_odd, near_ref[0, :, here], far_ref[0, :, here])
            image = image - jnp.where(plan_ref[at.flags + 2] != 0, 0.0, factor * before)
        if s == slices - 1:
            after = jnp.where(time_odd, far_ref[0, :, here], near_ref[0, :, here])
            image = image - jnp.where(plan_ref[at.flags + 3] != 0, 0.0, factor * after)
        new_ref[s] = image

    rows = at.rows + side * at.room
    tiles_at = at.tiles + side * 2 * at.room
    places = at.places + side * 2 * at.room

    def group(g, carry):
        done = []
        for k in range(GROUP):
            u = g * GROUP + k
            halves = [halves_ref[plan_ref[places + 2 * u + j]] for j in range(2)]
            tiles = [tiles_ref[plan_ref[tiles_at + 2 * u + j]] for j in range(2)]
            done.append((plan_ref[rows + u], product(halves, tiles, width)))
        for i, value in done:
            to = pl.ds(pl.multiple_of((i % half) * TILE, TILE), TILE)
            new_ref[i // half, :, to] += scale * value
        return carry

    lax.fori_loop(0, plan_ref[at.groups + side], group, 0)

    pair = (lambda other: (new_ref, other)) if side == 0 else (lambda other: (other, new_ref))
    if second and mode == "image":
        image_ref, left_ref, right_ref, matrix_ref = given
        mixed_ref, gram_ref = out_refs
        matrix = matrix_ref[...]
        gram, product_sum = 0.0, 0.0
        images = pair(image_ref)
        for s in range(slices):
            for k, y_ref in enumerate((left_ref, right_ref)):
                mixed = mix(matrix, y_ref[s])
                mixed_ref[s, :, k * points : (k + 1) * points] = mixed
                gram = gram + inner(mixed, mixed)
                product_sum = product_sum + inner(mixed, mix(matrix, images[k][s]))
        gram_ref[...] = folded(gram, product_sum)
    elif second:
        slice_ends(plan_ref[at.flags + 1], *pair(given[0]), *out_refs[:2])
        out_refs = out_refs[2:]
        if mode == "gram":
            gram = sum(inner(y[s], y[s]) for y in (given[0], new_ref) for s in range(slices))
            gram_ref = out_refs.pop(0)
            gram_ref[...] = folded(gram)
    if mode != "image" and out_refs:
        side_points = HB * TILE
        start = points - side_points if side else 0
        out_refs[0][...] = new_ref[:, :, start : start + side_points]


def folded(*matrices):
    width = matrices[0].shape[0]
    rows = width * width * len(matrices) // TILE
    flat = jnp.concatenate(matrices, axis=0)
    return jnp.concatenate([flat[i : i + rows] for i in range(0, flat.shape[0], rows)], axis=1)


def unfolded(block, width):
    rows = block.shape[0]
    flat = jnp.concatenate([block[:, i : i + width] for i in range(0, TILE, width)], axis=0)
    return [flat[i : i + width] for i in range(0, flat.shape[0], width)]


def finish(side, second, mode, scale, table, tiles, part, halo, ends, given=()):
    slices, width, points = part.shape
    ins = [table] + [near(v) for v in (tiles, part, halo, *ends, *given)]
    outs = [(part.shape, F32)]
    whole = (slices, width, 2 * points)
    if second and mode == "image":
        outs += [(whole, F32), ((2 * width * width // TILE, TILE), F32)]
    elif second:
        outs += [((1, width, 2 * points), F32)] * 2
        if mode == "gram":
            outs.append(((width * width // TILE, TILE), F32))
    if mode != "image" and points != HB * TILE:
        outs.append(((slices, width, HB * TILE), F32))
    return call(
        functools.partial(side_kernel, side, second, mode, scale),
        ins,
        outs,
        scratch=[VM((slices * HB + 1, 2 * width, TILE), BF16)],
        specs=[SCALARS] + [WHOLE] * (len(ins) - 1),
        flops=2 * slices * points * 4 * width * TILE * 2,
        moved=24 * part.size,
        name=("left_", "right_")[side] + mode,
        aliases={2: 0},
    )


def inverse_factor(gram):
    width = gram.shape[0]
    square = (width, width)
    rows = lax.broadcasted_iota(jnp.int32, square, 0)
    columns = lax.broadcasted_iota(jnp.int32, square, 1)
    inverse = (rows == columns).astype(F32)
    column = jnp.broadcast_to(gram[:, :1], square)
    for j in range(width - 1):
        following = jnp.broadcast_to(gram[:, j + 1 : j + 2], square)
        scaled = jnp.where(rows > j, column, 0.0) * (1.0 / column[j : j + 1])
        gram = gram - scaled * gram[j : j + 1]
        inverse = inverse - scaled * inverse[j : j + 1]
        column = following - scaled * column[j + 1 : j + 2]
    pivots = jnp.sum(jnp.where(rows == columns, gram, 0.0), axis=1, keepdims=True)
    return inverse * lax.rsqrt(pivots)


def factor_kernel(count, gram_ref, out_ref):
    (gram,) = unfolded(gram_ref[...] * (1.0 / count), out_ref.shape[0])
    out_ref[...] = inverse_factor(gram)


def factor(gram, width, count):
    return call(
        functools.partial(factor_kernel, float(count)),
        [near(gram)],
        [((width, width), F32)],
        specs=[WHOLE],
        flops=40000 * gram.size,
        moved=8 * gram.size,
        name="factor",
    )[0]


def basis_kernel(matrix_ref, left_ref, right_ref, out_ref):
    half = left_ref.shape[2]
    for s in range(left_ref.shape[0]):
        out_ref[s, :, :half] = mix(matrix_ref[...], left_ref[s])
        out_ref[s, :, half:] = mix(matrix_ref[...], right_ref[s])


def basis(matrix, ys):
    slices, width, half = ys[0].shape
    return call(
        basis_kernel,
        [near(matrix)] + [near(y) for y in ys],
        [((slices, width, 2 * half), F32)],
        specs=[WHOLE] * 3,
        flops=4 * width * ys[0].size,
        moved=16 * ys[0].size,
        name="basis",
        out_vmem=False,
    )[0]


def close_kernel(count, sums_ref, y_ref, basis_ref, ritz_ref):
    high = lax.Precision.HIGHEST
    gram, projected = unfolded(sums_ref[...] * (1.0 / count), ritz_ref.shape[0])
    matrix = inverse_factor(gram)
    for s in range(y_ref.shape[0]):
        basis_ref[s] = mix(matrix, y_ref[s])
    half = lax.dot_general(matrix, projected, NN, precision=high, preferred_element_type=F32)
    ritz_ref[...] = lax.dot_general(half, matrix, NT, precision=high, preferred_element_type=F32)


def close(sums, y, count):
    width = y.shape[1]
    return call(
        functools.partial(close_kernel, float(count)),
        [near(sums), near(y)],
        [(y.shape, F32), ((width, width), F32)],
        specs=[WHOLE] * 2,
        flops=2 * width * y.size,
        moved=8 * y.size,
        name="close",
        out_vmem=False,
    )


def stages_of(axis):
    count = lax.axis_size(axis)
    found, stride = [], 1
    if (count.bit_length() - 1) % 2:
        found, stride = [(axis, (1,))], 2
    while stride < count:
        found.append((axis, (stride, 2 * stride, 3 * stride)))
        stride *= 4
    return found


def pairs_of(axis):
    return [(axis, (1 << k,)) for k in range((lax.axis_size(axis) - 1).bit_length())]


def add_over(value, stages):
    for axis, strides in stages:
        count = lax.axis_size(axis)
        others = [lax.ppermute(value, axis, [(i, i ^ k) for i in range(count)]) for k in strides]
        if len(others) == 1:
            value = value + others[0]
        else:
            value = (value + others[0]) + (others[1] + others[2])
    return value


def inner_pairs(axis):
    count = lax.axis_size(axis)
    return [(i, i ^ 1) for i in range(count)]


def outer_pairs(axis):
    count = lax.axis_size(axis)
    return [(i, (i + 1) % count if i % 2 else (i - 1) % count) for i in range(count)]


def body(start_block, stiffness_tiles, tile_columns):
    slices, width, local_points = start_block.shape
    local_blocks = local_points // TILE
    blocks_all = lax.axis_size("space") * local_blocks
    count_all = slices * local_points * lax.axis_size("tm") * lax.axis_size("space")
    time_index = lax.axis_index("tm")
    ends = (time_index == 0, time_index == lax.axis_size("tm") - 1)
    space_index = lax.axis_index("space")
    odd = jnp.stack(
        [
            space_index % 2,
            time_index % 2,
            ends[0].astype(jnp.int32),
            ends[1].astype(jnp.int32),
            space_index * local_blocks,
        ]
    )

    left, right, *ends = start(odd, start_block)
    side = HB * TILE
    half = left.shape[2]
    state = ((left, right), ends, (left[:, :, :side], right[:, :, half - side :]))
    table = plan(tile_columns, odd, blocks_all)
    tiles = prep(stiffness_tiles)

    across, along = pairs_of("space"), pairs_of("tm")
    early = [along[:-1], along[-1:], across[:1], across[1:]]
    ring = lax.axis_size("space")
    up = [(i, (i + 1) % ring) for i in range(ring)]
    down = [((i + 1) % ring, i) for i in range(ring)]

    def step(mode, scale, first, state, previous=None, beside=None):
        halves, ends, sides = state
        halos = [None, None]
        for side in (first, 1 - first):
            pairs = down if side == 1 else up
            halos[side] = lax.ppermute(sides[1 - side], "space", pairs)
        far_slice = lax.ppermute(ends[1], "tm", outer_pairs("tm"))
        near_slice = lax.ppermute(ends[0], "tm", inner_pairs("tm"))
        ends = (near_slice, far_slice)
        parts = local_part(mode, scale, table, tiles, halves, previous)
        extra = None
        if beside is not None:
            parts, extra = lax.optimization_barrier((parts, beside[0]))
            extra = beside[1](extra)
        news, sends = [None, None], [None, None]
        new, *own = finish(first, False, mode, scale, table, tiles, parts[first], halos[first], ends)
        news[first], sends[first] = new, own[0] if own else new
        given = (new, *halves, extra) if mode == "image" else (new,)
        last = 1 - first
        part, _ = lax.optimization_barrier((parts[last], halos[first]))
        if beside is not None:
            part, extra = lax.optimization_barrier((part, extra))
        new, *rest = finish(last, True, mode, scale, table, tiles, part, halos[last], ends, given)
        if mode == "image":
            return rest[0], rest[1], extra
        ends, rest = rest[:2], rest[2:]
        gram = rest.pop(0) if mode == "gram" else None
        news[last], sends[last] = new, rest[0] if rest else new
        return (tuple(news), ends, sends), gram, extra

    def stage(n):
        return lambda gram: add_over(gram, early[n])

    state0 = state
    state1, _, _ = step("first", 1.0 / RADIUS, 0, state0)
    state2, _, _ = step("step", 2.0 / RADIUS, 1, state1, state0[0])
    filtered, gram, _ = step("gram", 2.0 / RADIUS, 0, state2, state1[0])
    state1, _, gram = step("first", 1.0 / RADIUS, 1, filtered, None, (gram, stage(0)))
    state2, _, gram = step("step", 2.0 / RADIUS, 0, state1, filtered[0], (gram, stage(1)))
    state3, _, gram = step("step", 2.0 / RADIUS, 1, state2, state1[0], (gram, stage(2)))
    second, sums, matrix = step(
        "image", 1.0, 0, state3, None, (gram, lambda gram: factor(stage(3)(gram), width, count_all))
    )
    first_basis = basis(matrix, filtered[0])
    sums = add_over(sums, stages_of("space") + stages_of("tm"))
    ritz_basis, ritz_matrix = close(sums, second, count_all)
    return ritz_basis, first_basis, ritz_matrix


def solution(mesh):
    placed = (P("tm", None, "space"), P("tm", "space", None, None), P("tm", "space"))
    return jax.shard_map(
        body,
        mesh=mesh,
        in_specs=placed,
        out_specs=(P("tm", None, "space"), P("tm", None, "space"), P()),
        check_vma=False,
    )
```
